32 devices in a mesh: row: 16 (over z, y, x), col: 2 (over core).
Axes of the slice: x: 2, y: 2, z: 4, core: 2. Of those that a mesh axis runs over, the one named last changes fastest.
Arguments:
- features: bfloat16 [128, 32, 16, 128], P('row', None, 'col'), may hold values from -6 to 6
- down_weight: bfloat16 [4, 4, 4, 32, 512], replicated, may hold values from -0.25 to 0.25
- bott_weight: bfloat16 [3, 3, 3, 512, 512], P(None, None, None, 'row'), may hold values from -0.078125 to 0.078125
- up_weight: bfloat16 [4, 4, 4, 32, 512], replicated, may hold values from -0.375 to 0.375
- dec_weight: bfloat16 [3, 3, 3, 32, 32], replicated, may hold values from -0.21875 to 0.21875
Outputs:
- decoded: bfloat16 [128, 32, 16, 128], P('row', None, 'col')
The draws below stay inside these ranges and needn't reach their ends.
All inputs are finite; a program needn't handle non-finite values.
Results may differ from the reference program's by a relative error of at most 0.015.
Values may be sent and summed in bfloat16 or wider, within the bound.
No kernel may reach another device: no remote copies, remote signals or barrier semaphores. Data moves between devices by JAX's collectives and lax.ppermute only.
A program may use at most 128 MiB of HBM per device.

```python
import jax
import jax.numpy as jnp
from jax import lax

C1 = 32
CB = 512
WIDTH = 128
DEPTH = 128
HEIGHT = 16


def steps_of(own_key, dims, split, least, top_value):
    gain = 1.0
    for dim, blocks in split:
        draws = jax.random.uniform(jax.random.fold_in(jax.random.fold_in(own_key, 6), dim), (blocks,), jnp.float32, least / len(split), top_value / len(split))
        gain = gain * jnp.repeat(jnp.exp(draws), dims[dim] // blocks).reshape((-1,) + (1,) * (len(dims) - 1 - dim))
    return gain


def normal_values(rng, dims, spread, most, shards=(), kind=jnp.bfloat16):
    level = steps_of(rng, dims, shards, -0.22, 0.18) if shards else 1.0
    values = jax.random.normal(rng, dims, jnp.float32) * spread * level
    return jnp.minimum(jnp.maximum(values, -most), most).astype(kind)


def setup_inputs(seed: int = 0) -> dict:
    key_list = jax.random.split(jax.random.key(seed), 6)
    features = normal_values(key_list[0], (DEPTH, C1, HEIGHT, WIDTH), 1.0, 6.0, ((0, 16), (2, 2)))
    down_weight = normal_values(key_list[1], (4, 4, 4, C1, CB), (16 * C1) ** -0.5, 0.25)
    bott_weight = normal_values(key_list[2], (3, 3, 3, CB, CB), (27 * CB // 2) ** -0.5, 0.078125, ((3, 16),))
    up_weight = normal_values(key_list[3], (4, 4, 4, C1, CB), (CB // 2) ** -0.5, 0.375)
    dec_weight = normal_values(key_list[4], (3, 3, 3, C1, C1), (27 * C1) ** -0.5, 0.21875)
    return {"features": features, "down_weight": down_weight, "bott_weight": bott_weight, "up_weight": up_weight, "dec_weight": dec_weight}


def convolve(field, kernel):
    return lax.conv_general_dilated(field[None].astype(jnp.float32), kernel.astype(jnp.float32), (1, 1, 1), ((1, 1), (1, 1), (1, 1)), dimension_numbers=("NDCHW", "DHWIO", "NDCHW"), precision=lax.Precision.HIGHEST, preferred_element_type=jnp.float32)[0]


def reference(features, down_weight, bott_weight, up_weight, dec_weight):
    depth, chans, height, width = features.shape
    pooled = features.astype(jnp.float32).reshape(depth // 2, 2, chans, height // 2, 2, width // 2, 2).mean(axis=(1, 4, 6)).astype(jnp.bfloat16)
    blocks = pooled.astype(jnp.float32).reshape(depth // 8, 4, chans, height // 8, 4, width // 8, 4)
    lowered = jax.nn.silu(jnp.einsum("daihbwc,abcio->dohw", blocks, down_weight.astype(jnp.float32), precision=lax.Precision.HIGHEST)).astype(jnp.bfloat16)
    middle = jax.nn.silu(convolve(lowered, bott_weight)).astype(jnp.bfloat16)
    raised = jnp.einsum("dihw,abcoi->daohbwc", middle.astype(jnp.float32), up_weight.astype(jnp.float32), precision=lax.Precision.HIGHEST)
    raised = raised.reshape(depth // 2, chans, height // 2, width // 2)
    raised = jnp.repeat(jnp.repeat(jnp.repeat(raised, 2, axis=0), 2, axis=2), 2, axis=3)
    joined = (features.astype(jnp.float32) + raised).astype(jnp.bfloat16)
    return jax.nn.silu(convolve(joined, dec_weight)).astype(jnp.bfloat16)
```

```python
import functools

import jax
import jax.numpy as jnp
from jax import lax
from jax.experimental import pallas as pl
from jax.experimental.pallas import tpu as pltpu
from jax.sharding import PartitionSpec as P

F32, BF16 = jnp.float32, jnp.bfloat16
NT = (((1,), (1,)), ((), ()))


def iota(shape, dim):
    return lax.broadcasted_iota(jnp.int32, shape, dim)


def dot(a, b):
    return jnp.dot(a, b, preferred_element_type=F32)


def dot_nt(a, b):
    return lax.dot_general(a, b, NT, preferred_element_type=F32)


def silu(v):
    return v / (1.0 + jnp.exp(-v))


def lower_kernel(count, chans, height, feat, down, out):
    planes, rows, width = feat.shape
    coarse = width // 8
    half = height // 2
    each = down.shape[4] // count
    shape = (half * chans, rows)
    r, c = iota(shape, 0), iota(shape, 1)
    pick = ((r % chans == c // height) & (r // chans == (c % height) // 2)).astype(F32).astype(BF16)
    sums = []
    for a in range(planes // 2):
        sums.append((dot(pick, feat[2 * a]) + dot(pick, feat[2 * a + 1])).astype(BF16))
    table = jnp.concatenate(sums, axis=0)
    shape = (4 * coarse, width)
    r, c = iota(shape, 0), iota(shape, 1)
    cols = ((r % coarse == c // 8) & (r // coarse == (c % 8) // 2)).astype(F32).astype(BF16)
    pooled = (dot_nt(cols, table) * 0.125).astype(BF16)
    low = jnp.zeros((coarse, down.shape[4]), F32)
    for c in range(4):
        weight = down[:, :, c].reshape(-1, down.shape[4])
        low = low + dot(pooled[c * coarse : (c + 1) * coarse], weight)
    low = silu(low)
    place = iota(low.shape, 0)
    before = jnp.where(place == 0, 0.0, pltpu.roll(low, 1, 0))
    after = jnp.where(place == coarse - 1, 0.0, pltpu.roll(low, coarse - 1, 0))
    for k in range(count):
        part = slice(k * each, (k + 1) * each)
        out[k] = jnp.concatenate([before[:, part], low[:, part], after[:, part]], axis=1).astype(BF16)


def bottleneck_kernel(sides, taps_of, *refs):
    blocks, weight, out, pads = refs[:sides], refs[sides], refs[sides + 1], refs[sides + 2 :]
    depth, coarse, lanes = blocks[0].shape
    rows = depth * coarse
    total = jnp.zeros((rows, weight.shape[4]), F32)
    taps = taps_of()
    for block, tap, pad in zip(blocks, taps, pads):
        zero = jnp.zeros((coarse, lanes), BF16)
        pad[:coarse] = zero
        pad[coarse + rows :] = zero
        pad[coarse : coarse + rows] = block[...].reshape(rows, lanes)
        for a in range(3):
            kernel = weight[a, tap].reshape(lanes, weight.shape[4])
            total = total + dot(pad[a * coarse : a * coarse + rows], kernel)
    out[...] = total.astype(BF16).reshape(out.shape)


def raise_kernel(chans, height, parts, feat, up, joined, spread):
    planes, rows, width = feat.shape
    coarse = width // 8
    total = parts[0].astype(F32)
    for k in range(1, parts.shape[0]):
        total = total + parts[k].astype(F32)
    middle = silu(total).astype(BF16)
    shape = (4 * width, coarse)
    r, c = iota(shape, 0), iota(shape, 1)
    pick = (((r % width) // 8 == c) & ((r % 8) // 2 == r // width)).astype(F32).astype(BF16)
    wide = dot(pick, middle).astype(BF16)
    raised = None
    for c in range(4):
        weight = up[:, :, c].reshape(-1, up.shape[4])
        term = dot_nt(weight, wide[c * width : (c + 1) * width])
        raised = term if raised is None else raised + term
    per = chans * (height // 2)
    for d in range(planes):
        spread[...] = feat[d].astype(F32)
        for h in range(height):
            start = (d // 2) * per + (h // 2) * chans
            value = spread[pl.ds(h, chans, stride=height), :] + raised[start : start + chans]
            joined[d, h * chans : (h + 1) * chans] = value.astype(BF16)


def band_kernel(chans, height, dec, out):
    eye = (iota((chans, chans), 0) == iota((chans, chans), 1)).astype(F32).astype(BF16)
    span = (height + 2) * chans
    total = 3 * span
    wide = -(-total // 128) * 128
    for c in range(3):
        taps = dot_nt(eye, dec[:, :, c].reshape(9 * chans, chans))
        pieces = []
        for a in range(3):
            pieces.append(taps[:, a * 3 * chans : (a + 1) * 3 * chans])
            pieces.append(jnp.zeros((chans, span - 3 * chans), F32))
        pieces.append(jnp.zeros((chans, wide - total), F32))
        base = jnp.concatenate(pieces, axis=1)
        for h in range(height):
            row = (c * height + h) * chans
            moved = base if h == 0 else pltpu.roll(base, h * chans, 1)
            out[row : row + chans] = moved[:, :total].astype(BF16)


def decode_kernel(chans, height, band, joined, low_h, high_h, low_d, high_d, out, field, spread):
    planes, rows, width = joined.shape
    span = rows + 2 * chans
    field[:span] = low_d[...]
    for d in range(planes):
        at = (d + 1) * span
        field[at : at + chans] = low_h[d]
        field[at + chans : at + chans + rows] = joined[d]
        field[at + chans + rows : at + span] = high_h[d]
    field[(planes + 1) * span :] = high_d[...]
    lane = iota((rows, width), 1)

    def pair(step, carry):
        at = pl.multiple_of(step * 2 * span, 16)
        window = jnp.concatenate(
            [field[pl.ds(at, 3 * span)], field[pl.ds(at + span, 3 * span)]], axis=1
        )
        sums = dot(band[...], window)
        for e in range(2):
            part = sums[:, e * width : (e + 1) * width]
            before = jnp.where(lane == 0, 0.0, pltpu.roll(part[:rows], 1, 1))
            after = jnp.where(lane == width - 1, 0.0, pltpu.roll(part[2 * rows :], width - 1, 1))
            value = silu(part[rows : 2 * rows] + before + after)
            for h in range(height):
                spread[pl.ds(h, chans, stride=height), :] = value[h * chans : (h + 1) * chans]
            out[step * 2 + e] = spread[...].astype(BF16)
        return carry

    lax.fori_loop(0, planes // 2, pair, 0)


def call(kernel, shape, scratch=(), name=None, flops=0, nbytes=0):
    return pl.pallas_call(
        kernel,
        out_shape=shape,
        scratch_shapes=list(scratch),
        name=name,
        cost_estimate=pl.CostEstimate(flops=flops, bytes_accessed=nbytes, transcendentals=0),
        compiler_params=pltpu.CompilerParams(vmem_limit_bytes=40 << 20),
    )


def bf16(*shape):
    return jax.ShapeDtypeStruct(shape, BF16)


def swap_pairs(count):
    first = [(i, i ^ 1) for i in range(count)]
    second = [(i, (i + 1 if i % 2 else i - 1) % count) for i in range(count)]
    return first, second


def body(features, down_weight, bott_weight, up_weight, dec_weight):
    depth, chans, height, width = features.shape
    count, cols = lax.axis_size("row"), lax.axis_size("col")
    top = down_weight.shape[4]
    coarse, rows, each = width // 8, chans * height, bott_weight.shape[3]
    feat = features.reshape(depth, rows, width)
    row, col = lax.axis_index("row"), lax.axis_index("col")

    lowered = call(
        functools.partial(lower_kernel, count, chans, height), bf16(count, coarse, 3 * each), name="lower"
    )(feat, down_weight)
    own = lax.all_to_all(lowered, "row", split_axis=0, concat_axis=0, tiled=True)

    up_one = [(i, i + 1) for i in range(cols - 1)]
    down_one = [(i + 1, i) for i in range(cols - 1)]
    if cols == 2:
        blocks = [own, lax.ppermute(own, "col", up_one + down_one)]
        taps_of = lambda: (1, 2 - 2 * lax.axis_index("col"))
    else:
        blocks = [lax.ppermute(own, "col", up_one), own, lax.ppermute(own, "col", down_one)]
        taps_of = lambda: (0, 1, 2)
    shares = call(
        functools.partial(bottleneck_kernel, len(blocks), taps_of),
        bf16(count, coarse, top),
        scratch=[pltpu.VMEM(((count + 2) * coarse, 3 * each), BF16) for _ in blocks],
        name="bottleneck",
    )(*blocks, bott_weight)
    parts = lax.all_to_all(shares, "row", split_axis=0, concat_axis=0, tiled=True)

    joined = call(
        functools.partial(raise_kernel, chans, height),
        bf16(depth, rows, width),
        scratch=[pltpu.VMEM((rows, width), F32)],
        name="raise",
    )(parts, feat, up_weight)

    span = 3 * (rows + 2 * chans)
    band = call(
        functools.partial(band_kernel, chans, height), bf16(3 * rows, span), name="band"
    )(dec_weight)

    bottom, top_rows = joined[:, :chans], joined[:, rows - chans :]
    none = jnp.zeros_like(bottom)
    if cols == 2:
        other = lax.ppermute(jnp.where(col == 0, top_rows, bottom), "col", up_one + down_one)
        low_h = jnp.where(col == 0, none, other)
        high_h = jnp.where(col == 0, other, none)
    else:
        low_h = lax.ppermute(top_rows, "col", up_one)
        high_h = lax.ppermute(bottom, "col", down_one)
    first = jnp.concatenate([low_h[0], joined[0], high_h[0]], axis=0)
    last = jnp.concatenate([low_h[-1], joined[-1], high_h[-1]], axis=0)
    if count % 2 == 0:
        even = row % 2 == 0
        pairs, others = swap_pairs(count)
        near = lax.ppermute(jnp.where(even, last, first), "row", pairs)
        far = lax.ppermute(jnp.where(even, first, last), "row", others)
        low_d = jnp.where(row == 0, jnp.zeros_like(first), jnp.where(even, far, near))
        high_d = jnp.where(row == count - 1, jnp.zeros_like(first), jnp.where(even, near, far))
    else:
        low_d = lax.ppermute(last, "row", [(i, i + 1) for i in range(count - 1)])
        high_d = lax.ppermute(first, "row", [(i + 1, i) for i in range(count - 1)])

    decoded = call(
        functools.partial(decode_kernel, chans, height),
        bf16(depth, rows, width),
        scratch=[
            pltpu.VMEM(((depth + 2) * (rows + 2 * chans), width), BF16),
            pltpu.VMEM((rows, width), F32),
        ],
        name="decode",
    )(band, joined, low_h, high_h, low_d, high_d)
    return decoded.reshape(depth, chans, height, width)


def solution(mesh):
    placed = (P("row", None, "col", None), P(), P(None, None, None, "row", None), P(), P())
    return jax.shard_map(
        body, mesh=mesh, in_specs=placed, out_specs=P("row", None, "col", None), check_vma=False
    )
```

```python
import functools

import jax
import jax.numpy as jnp
from jax import lax
from jax.experimental import pallas as pl
from jax.experimental.pallas import tpu as pltpu
from jax.sharding import PartitionSpec as P

F32, BF16 = jnp.float32, jnp.bfloat16
NT = (((1,), (1,)), ((), ()))


def iota(shape, dim):
    return lax.broadcasted_iota(jnp.int32, shape, dim)


def dot(a, b):
    return jnp.dot(a, b, preferred_element_type=F32)


def dot_nt(a, b):
    return lax.dot_general(a, b, NT, preferred_element_type=F32)


def silu(v):
    half = 0.5 * v
    return half + half * jnp.tanh(half)


def lower_kernel(count, repeat, chans, height, feat_hbm, down_hbm, out, feat, down, sems):
    planes, rows, width = feat.shape
    quarters = planes // 2
    loads = [
        pltpu.make_async_copy(feat_hbm.at[2 * a : 2 * a + 2], feat.at[2 * a : 2 * a + 2], sems.at[a])
        for a in range(quarters)
    ] + [
        pltpu.make_async_copy(down_hbm.at[a], down.at[a], sems.at[quarters + a]) for a in range(quarters)
    ]
    for load in loads:
        load.start()
    coarse = width // 8
    half = height // 2
    top = down.shape[4]
    each = top // count
    shape = (half * chans, rows)
    r, c = iota(shape, 0), iota(shape, 1)
    pick = ((r % chans == c // height) & (r // chans == (c % height) // 2)).astype(F32).astype(BF16)
    shape = (4 * coarse, width)
    r, c = iota(shape, 0), iota(shape, 1)
    cols = ((r % coarse == c // 8) & (r // coarse == (c % 8) // 2)).astype(F32).astype(BF16)
    for a in range(quarters):
        loads[a].wait()
    tables = [(dot(pick, feat[2 * a]) + dot(pick, feat[2 * a + 1])).astype(BF16) for a in range(quarters)]
    pooled = [(dot_nt(cols, table) * 0.125).astype(BF16) for table in tables]
    low = jnp.zeros((coarse, top), F32)
    for a in range(quarters):
        loads[quarters + a].wait()
        for c in range(4):
            low = low + dot(pooled[a][c * coarse : (c + 1) * coarse], down[a, :, c].reshape(-1, top))
    low = silu(low)
    place = iota(low.shape, 0)
    before = jnp.where(place == 0, 0.0, pltpu.roll(low, 1, 0))
    after = jnp.where(place == coarse - 1, 0.0, pltpu.roll(low, coarse - 1, 0))
    for k in range(count):
        part = slice(k * each, (k + 1) * each)
        block = jnp.concatenate([before[:, part], low[:, part], after[:, part]], axis=1).astype(BF16)
        for e in range(repeat):
            out[repeat * k + e] = block


def bottleneck_kernel(joint, blocks, *refs):
    if joint:
        got, weight, out = refs[:3]
        pads = refs[3:]
        col = lax.axis_index("col")
        sources = [(got[:, col], 1), (got[:, 1 - col], 2 - 2 * col)]
    else:
        weight, out = refs[blocks : blocks + 2]
        pads = refs[blocks + 2 :]
        sources = [(refs[k][...], k) for k in range(blocks)]
    depth, coarse, top = out.shape
    rows = depth * coarse
    lanes = 3 * weight.shape[3]
    total = jnp.zeros((rows, top), F32)
    for (block, tap), pad in zip(sources, pads):
        zero = jnp.zeros((coarse, lanes), BF16)
        pad[:coarse] = zero
        pad[coarse + rows :] = zero
        pad[coarse : coarse + rows] = block.reshape(rows, lanes)
        for a in range(3):
            kernel = weight[a, tap].reshape(lanes, top)
            total = total + dot(pad[a * coarse : a * coarse + rows], kernel)
    out[...] = total.astype(BF16).reshape(out.shape)


def raise_kernel(chans, height, parts, feat, up, joined, ends, *rest):
    sides, spread = rest[:-1], rest[-1]
    planes, rows, width = feat.shape
    coarse = width // 8
    total = parts[0].astype(F32)
    for k in range(1, parts.shape[0]):
        total = total + parts[k].astype(F32)
    middle = silu(total).astype(BF16)
    shape = (4 * width, coarse)
    r, c = iota(shape, 0), iota(shape, 1)
    pick = (((r % width) // 8 == c) & ((r % 8) // 2 == r // width)).astype(F32).astype(BF16)
    wide = dot(pick, middle).astype(BF16)
    raised = None
    for c in range(4):
        weight = up[:, :, c].reshape(-1, up.shape[4])
        term = dot_nt(weight, wide[c * width : (c + 1) * width])
        raised = term if raised is None else raised + term
    per = chans * (height // 2)
    for d in range(planes):
        spread[d] = feat[d].astype(F32)
        for h in range(height):
            start = (d // 2) * per + (h // 2) * chans
            value = spread[d, pl.ds(h, chans, stride=height), :] + raised[start : start + chans]
            joined[d, h * chans : (h + 1) * chans] = value.astype(BF16)
    odd = lax.axis_index("row") % 2
    near, far = (planes - 1) * (1 - odd), (planes - 1) * odd
    ends[0] = joined[near]
    ends[1] = joined[far]
    if len(sides) == 1:
        starts = [pl.multiple_of((rows - chans) * (1 - lax.axis_index("col")), chans)]
    else:
        starts = [0, rows - chans]
    for side, start in zip(sides, starts):
        for d in range(planes):
            side[d] = joined[d, pl.ds(start, chans)]
        side[planes] = joined[near, pl.ds(start, chans)]
        side[planes + 1] = joined[far, pl.ds(start, chans)]


def band_kernel(chans, height, dec, after, out):
    eye = (iota((chans, chans), 0) == iota((chans, chans), 1)).astype(F32).astype(BF16)
    step = 3 * chans
    wide = out.shape[1]
    for c in range(3):
        taps = [dot_nt(eye, dec[:, b, c].reshape(step, chans)) for b in range(3)]
        base = jnp.concatenate(taps + [jnp.zeros((chans, wide - 3 * step), F32)], axis=1)
        for h in range(height):
            row = h * step + c * chans
            moved = base if h == 0 else pltpu.roll(base, h * step, 1)
            out[row : row + chans] = moved.astype(BF16)


def decode_pair(chans, height, band, planes, spread, store):
    step = 3 * chans
    blocks = [jnp.concatenate([plane(h) for plane in planes], axis=1) for h in range(height + 2)]
    window = jnp.concatenate(blocks, axis=0)
    width = window.shape[1] // 2
    sums = [None] * height
    for at in range(0, window.shape[0], 256):
        stop = min(at + 256, window.shape[0])
        first = max(0, at // step - 2)
        last = min(height - 1, (stop - 1) // step)
        part = dot(band[first * step : (last + 1) * step, at:stop], window[at:stop])
        for h in range(first, last + 1):
            piece = part[(h - first) * step : (h - first + 1) * step]
            sums[h] = piece if sums[h] is None else sums[h] + piece
    lane = iota((chans, width), 1)
    for e in range(2):
        for h in range(height):
            part = sums[h][:, e * width : (e + 1) * width]
            before = jnp.where(lane == 0, 0.0, pltpu.roll(part[:chans], 1, 1))
            after = jnp.where(lane == width - 1, 0.0, pltpu.roll(part[2 * chans :], width - 1, 1))
            spread[e, pl.ds(h, chans, stride=height), :] = silu(part[chans : 2 * chans] + before + after)
        store(e, spread[e].astype(BF16))


def fill(field, slot, chans, plane, borders):
    height = field.shape[0]
    at = slice(slot * chans, (slot + 1) * chans)
    for h in range(1, height - 1):
        field[h, at] = plane[(h - 1) * chans : h * chans]
    if len(borders) == 1:
        col = lax.axis_index("col")
        field[(height - 1) * col, at] = jnp.zeros_like(borders[0])
        field[(height - 1) * (1 - col), at] = borders[0]
    else:
        field[0, at] = borders[0]
        field[height - 1, at] = borders[1]


def interior_kernel(chans, height, band, joined, *rest):
    sides, (out_hbm, field, spread, held, sems) = rest[:-5], rest[-5:]
    planes = joined.shape[0]
    for d in range(planes):
        fill(field, d, chans, joined[d], [side[d] for side in sides])
    copies = []
    for step in range(planes // 2 - 1):
        views = [
            lambda h, at=(2 * step + e) * chans: field[h, at : at + 3 * chans] for e in range(2)
        ]

        def store(e, value):
            held[2 * step + e] = value

        decode_pair(chans, height, band, views, spread.at[step], store)
        copies.append(
            pltpu.make_async_copy(
                held.at[2 * step : 2 * step + 2], out_hbm.at[2 * step + 1 : 2 * step + 3], sems.at[step]
            )
        )
        copies[-1].start()
    for copy in copies:
        copy.wait()


def edge_kernel(chans, height, band, joined, near, far, *rest):
    sides, (mid_hbm, out_hbm, field, spread, held, sems) = rest[:-6], rest[-6:]
    planes, rows, width = joined.shape
    for slot, d in ((1, 0), (2, 1), (3, planes - 2), (4, planes - 1)):
        fill(field, slot, chans, joined[d], [side[d] for side in sides])
    row, last = lax.axis_index("row"), lax.axis_size("row") - 1

    def outer(slot, got):
        borders = [got[rows + k * chans : rows + (k + 1) * chans] for k in range(len(sides))]
        fill(field, slot, chans, got[:rows], borders)

    @pl.when(row % 2 == 0)
    def _():
        outer(0, far[...])
        outer(5, near[...])

    @pl.when(row % 2 == 1)
    def _():
        outer(0, near[...])
        outer(5, far[...])

    @pl.when(row == 0)
    def _():
        field[:, :chans] = jnp.zeros((height + 2, chans, width), BF16)

    @pl.when(row == last)
    def _():
        field[:, 5 * chans :] = jnp.zeros((height + 2, chans, width), BF16)

    copies = [
        pltpu.make_async_copy(held.at[e], out_hbm.at[d], sems.at[e]) for e, d in ((0, 0), (1, planes - 1))
    ]

    def store(e, value):
        held[e] = value
        copies[e].start()

    views = [lambda h, at=3 * e * chans: field[h, at : at + 3 * chans] for e in range(2)]
    decode_pair(chans, height, band, views, spread, store)
    for copy in copies:
        copy.wait()


VMEM = pl.BlockSpec(memory_space=pltpu.MemorySpace.VMEM)
HBM = pl.BlockSpec(memory_space=pltpu.MemorySpace.HBM)


def fixed(x):
    return pltpu.with_memory_space_constraint(x, pltpu.MemorySpace.HBM)


def call(kernel, name, shape, ins, out, scratch=(), aliases=None, cost=0, limit=24):
    return pl.pallas_call(
        kernel,
        out_shape=shape,
        in_specs=ins,
        out_specs=out,
        scratch_shapes=list(scratch),
        input_output_aliases=aliases or {},
        name=name,
        cost_estimate=pl.CostEstimate(flops=cost, bytes_accessed=cost // 100, transcendentals=0),
        compiler_params=pltpu.CompilerParams(vmem_limit_bytes=limit << 20),
    )


def bf16(*shape):
    return jax.ShapeDtypeStruct(shape, BF16)


def neighbour_swaps(count, cols):
    ids = lambda row, col: row * cols + col
    first = [(ids(r, c), ids(r ^ 1, c)) for r in range(count) for c in range(cols)]
    second = []
    for r in range(count):
        for c in range(cols):
            other = r + 1 if r % 2 else r - 1
            inside = 0 <= other < count
            second.append((ids(r, c), ids(other, c) if inside else ids(r, c ^ 1)))
    return first, second


def body(features, down_weight, bott_weight, up_weight, dec_weight):
    depth, chans, height, width = features.shape
    count, cols = lax.axis_size("row"), lax.axis_size("col")
    top = down_weight.shape[4]
    coarse, rows, each = width // 8, chans * height, bott_weight.shape[3]
    feat = features.reshape(depth, rows, width)

    sems = lambda n: pltpu.SemaphoreType.DMA((n,))
    lower = functools.partial(lower_kernel, count, 2 if cols == 2 else 1, chans, height)
    lowered = call(
        lower,
        "lower",
        bf16((2 if cols == 2 else 1) * count, coarse, 3 * each),
        [HBM, HBM],
        VMEM,
        [pltpu.VMEM(feat.shape, BF16), pltpu.VMEM(down_weight.shape, BF16), sems(depth)],
        limit=24, cost=1_000_000_000,
    )(fixed(feat), fixed(down_weight))
    up_one = [(i, i + 1) for i in range(cols - 1)]
    down_one = [(i + 1, i) for i in range(cols - 1)]
    if cols == 2:
        got = lax.all_to_all(lowered, ("row", "col"), split_axis=0, concat_axis=0, tiled=True)
        blocks = [got.reshape(count, cols, coarse, 3 * each)]
        sides = 2
    else:
        own = lax.all_to_all(lowered, "row", split_axis=0, concat_axis=0, tiled=True)
        blocks = [lax.ppermute(own, "col", up_one), own, lax.ppermute(own, "col", down_one)]
        sides = 3
    shares = call(
        functools.partial(bottleneck_kernel, cols == 2, sides),
        "bottleneck",
        bf16(count, coarse, top),
        [VMEM] * (len(blocks) + 1),
        VMEM,
        [pltpu.VMEM(((count + 2) * coarse, 3 * each), BF16) for _ in range(sides)],
        cost=2_000_000_000,
    )(*blocks, bott_weight)
    parts = lax.all_to_all(shares, "row", split_axis=0, concat_axis=0, tiled=True)

    side = bf16(depth + 2, chans, width)
    sides = 1 if cols == 2 else 2
    joined, ends, *sides = call(
        functools.partial(raise_kernel, chans, height),
        "raise",
        (bf16(depth, rows, width), bf16(2, rows, width)) + (side,) * sides,
        [VMEM] * 3,
        (VMEM,) * (2 + sides),
        [pltpu.VMEM(feat.shape, F32)],
    )(parts, feat, up_weight)
    if cols == 2:
        sides = [lax.ppermute(sides[0], "col", up_one + down_one)]
    else:
        sides = [lax.ppermute(sides[1], "col", up_one), lax.ppermute(sides[0], "col", down_one)]

    span = rows + 2 * chans
    band = call(
        functools.partial(band_kernel, chans, height),
        "band",
        bf16(3 * rows, -(-3 * span // 128) * 128),
        [VMEM, HBM],
        VMEM,
        cost=500_000_000,
    )(dec_weight, joined)

    got = []
    for k, pairs in enumerate(neighbour_swaps(count, cols)):
        sent = jnp.concatenate([ends[k]] + [side[depth + k] for side in sides], axis=0)
        got.append(lax.ppermute(sent, ("row", "col"), pairs))

    shape = bf16(depth, rows, width)
    inner = call(
        functools.partial(interior_kernel, chans, height),
        "interior",
        shape,
        [VMEM] * (2 + len(sides)),
        HBM,
        [
            pltpu.VMEM((height + 2, depth * chans, width), BF16),
            pltpu.VMEM((depth // 2 - 1, 2, rows, width), F32),
            pltpu.VMEM((depth - 2, rows, width), BF16),
            sems(depth // 2 - 1),
        ],
        cost=3_000_000_000,
    )(band, joined, *sides)
    decoded = call(
        functools.partial(edge_kernel, chans, height),
        "edge",
        shape,
        [VMEM] * (4 + len(sides)) + [HBM],
        HBM,
        [
            pltpu.VMEM((height + 2, 6 * chans, width), BF16),
            pltpu.VMEM((2, rows, width), F32),
            pltpu.VMEM((2, rows, width), BF16),
            sems(2),
        ],
        aliases={4 + len(sides): 0},
        cost=1_000_000_000,
    )(band, joined, *got, *sides, inner)
    return decoded.reshape(depth, chans, height, width)


def solution(mesh):
    placed = (P("row", None, "col", None), P(), P(None, None, None, "row", None), P(), P())
    return jax.shard_map(
        body, mesh=mesh, in_specs=placed, out_specs=P("row", None, "col", None), check_vma=False
    )
```

```python
import functools

import jax
import jax.numpy as jnp
from jax import lax
from jax.experimental import pallas as pl
from jax.experimental.pallas import tpu as pltpu
from jax.sharding import PartitionSpec as P

F32, BF16 = jnp.float32, jnp.bfloat16
NT = (((1,), (1,)), ((), ()))


def iota(shape, dim):
    return lax.broadcasted_iota(jnp.int32, shape, dim)


def dot(a, b):
    return jnp.dot(a, b, preferred_element_type=F32)


def dot_nt(a, b):
    return lax.dot_general(a, b, NT, preferred_element_type=F32)


def silu(v):
    half = 0.5 * v
    return half + half * jnp.tanh(half)


def lowered_rows(height, chans, loads, feat, down):
    planes, rows, width = feat.shape
    quarters = planes // 2
    coarse = width // 8
    top = down.shape[4]
    shape = (height // 2 * chans, rows)
    r, c = iota(shape, 0), iota(shape, 1)
    pick = ((r % chans == c // height) & (r // chans == (c % height) // 2)).astype(F32).astype(BF16)
    shape = (4 * coarse, width)
    r, c = iota(shape, 0), iota(shape, 1)
    cols = ((r % coarse == c // 8) & (r // coarse == (c % 8) // 2)).astype(F32).astype(BF16)
    for a in range(quarters):
        loads[a].wait()
    tables = [(dot(pick, feat[2 * a]) + dot(pick, feat[2 * a + 1])).astype(BF16) for a in range(quarters)]
    pooled = [(dot_nt(cols, table) * 0.125).astype(BF16) for table in tables]
    low = jnp.zeros((coarse, top), F32)
    for a in range(quarters):
        loads[quarters + a].wait()
        for c in range(4):
            low = low + dot(pooled[a][c * coarse : (c + 1) * coarse], down[a, :, c].reshape(-1, top))
    return silu(low)


def input_loads(feat_hbm, down_hbm, feat, down, sems):
    quarters = feat.shape[0] // 2
    return [
        pltpu.make_async_copy(feat_hbm.at[2 * a : 2 * a + 2], feat.at[2 * a : 2 * a + 2], sems.at[a])
        for a in range(quarters)
    ] + [
        pltpu.make_async_copy(down_hbm.at[a], down.at[a], sems.at[quarters + a]) for a in range(quarters)
    ]


def lower_kernel(count, chans, height, feat_hbm, down_hbm, out, feat, down, sems):
    loads = input_loads(feat_hbm, down_hbm, feat, down, sems)
    for load in loads:
        load.start()
    low = lowered_rows(height, chans, loads, feat, down)
    coarse = low.shape[0]
    each = low.shape[1] // count
    place = iota(low.shape, 0)
    before = jnp.where(place == 0, 0.0, pltpu.roll(low, 1, 0))
    after = jnp.where(place == coarse - 1, 0.0, pltpu.roll(low, coarse - 1, 0))
    for k in range(count):
        part = slice(k * each, (k + 1) * each)
        out[k] = jnp.concatenate([before[:, part], low[:, part], after[:, part]], axis=1).astype(BF16)


def quarter(row, col, size):
    return pl.multiple_of((2 * (row % 2) + col) * size, size)


def lower_pair_kernel(count, chans, height, feat_hbm, down_hbm, bott_hbm, out, keep, give, feat, down, sems):
    loads = input_loads(feat_hbm, down_hbm, feat, down, sems)
    row, col = lax.axis_index("row"), lax.axis_index("col")
    size = keep.shape[4]
    quarters = [
        pltpu.make_async_copy(
            bott_hbm.at[:, :, :, :, pl.ds(quarter(owner, col, size), size)], held, sems.at[len(loads) + k]
        )
        for k, (owner, held) in enumerate(((row + 1, give), (row, keep)))
    ]
    for load in loads + quarters:
        load.start()
    low = lowered_rows(height, chans, loads, feat, down)
    half = low.shape[0] // 2
    each = low.shape[1] // count
    for k in range(count):
        pieces = []
        for rows in (slice(0, half), slice(half, 2 * half)):
            for owner in (k, k ^ 1):
                pieces.append(low[rows, owner * each : (owner + 1) * each])
        block = jnp.concatenate(pieces, axis=1).astype(BF16)
        out[2 * k] = block
        out[2 * k + 1] = block
    for load in quarters:
        load.wait()


def bottleneck_kernel(*refs):
    blocks, weight, out, pads = refs[:3], refs[3], refs[4], refs[5:]
    depth, coarse, top = out.shape
    rows = depth * coarse
    lanes = 3 * weight.shape[3]
    total = jnp.zeros((rows, top), F32)
    for tap, (block, pad) in enumerate(zip(blocks, pads)):
        zero = jnp.zeros((coarse, lanes), BF16)
        pad[:coarse] = zero
        pad[coarse + rows :] = zero
        pad[coarse : coarse + rows] = block[...].reshape(rows, lanes)
        for a in range(3):
            kernel = weight[a, tap].reshape(lanes, top)
            total = total + dot(pad[a * coarse : a * coarse + rows], kernel)
    out[...] = total.astype(BF16).reshape(out.shape)


def bottleneck_pair_kernel(got, keep, took, out, pad):
    depth, _, half, lanes = got.shape
    group = lanes // 2
    coarse = 2 * half
    rows = depth * coarse
    lane = iota((half, lanes), 1)
    blocks = []
    for d in range(depth):
        low, high = got[d, 0].astype(F32), got[d, 1].astype(F32)
        blocks.append(jnp.where(lane < group, low, pltpu.roll(high, group, 1)))
        blocks.append(jnp.where(lane < group, pltpu.roll(low, group, 1), high))
    here = jnp.concatenate(blocks, axis=0)
    place = iota((rows, lanes), 0) % coarse
    before = jnp.where(place == 0, 0.0, pltpu.roll(here, 1, 0))
    after = jnp.where(place == coarse - 1, 0.0, pltpu.roll(here, rows - 1, 0))
    zero = jnp.zeros((coarse, 3 * lanes), BF16)
    pad[:coarse] = zero
    pad[coarse + rows :] = zero
    for c, value in enumerate((before, here, after)):
        pad[coarse : coarse + rows, c * lanes : (c + 1) * lanes] = value.astype(BF16)
    total = None
    for a in range(3):
        bands = []
        for c in range(3):
            for source in range(2):
                for held in (keep, took):
                    bands.append(jnp.concatenate([held[a, source - h + 1, c] for h in range(2)], axis=1))
        term = dot(pad[a * coarse : a * coarse + rows], jnp.concatenate(bands, axis=0))
        total = term if total is None else total + term
    size = out.shape[2]
    for h in range(2):
        for d in range(depth):
            out[2 * d + h] = total[d * coarse : (d + 1) * coarse, h * size : (h + 1) * size].astype(BF16)


def raise_kernel(chans, height, parts, feat, up, joined, ends, *rest):
    sides, spread = rest[:-1], rest[-1]
    planes, rows, width = feat.shape
    coarse = width // 8
    groups = up.shape[4] // parts.shape[2]
    sums = []
    for q in range(groups):
        total = parts[q].astype(F32)
        for k in range(q + groups, parts.shape[0], groups):
            total = total + parts[k].astype(F32)
        sums.append(total)
    middle = silu(sums[0] if groups == 1 else jnp.concatenate(sums, axis=1)).astype(BF16)
    shape = (4 * width, coarse)
    r, c = iota(shape, 0), iota(shape, 1)
    pick = (((r % width) // 8 == c) & ((r % 8) // 2 == r // width)).astype(F32).astype(BF16)
    wide = dot(pick, middle).astype(BF16)
    raised = None
    for c in range(4):
        weight = up[:, :, c].reshape(-1, up.shape[4])
        term = dot_nt(weight, wide[c * width : (c + 1) * width])
        raised = term if raised is None else raised + term
    per = chans * (height // 2)
    for d in range(planes):
        spread[d] = feat[d].astype(F32)
        for h in range(height):
            start = (d // 2) * per + (h // 2) * chans
            value = spread[d, pl.ds(h, chans, stride=height), :] + raised[start : start + chans]
            joined[d, h * chans : (h + 1) * chans] = value.astype(BF16)
    odd = lax.axis_index("row") % 2
    near, far = (planes - 1) * (1 - odd), (planes - 1) * odd
    ends[0] = joined[near]
    ends[1] = joined[far]
    if len(sides) == 1:
        starts = [pl.multiple_of((rows - chans) * (1 - lax.axis_index("col")), chans)]
    else:
        starts = [0, rows - chans]
    for side, start in zip(sides, starts):
        for d in range(planes):
            side[d] = joined[d, pl.ds(start, chans)]
        side[planes] = joined[near, pl.ds(start, chans)]
        side[planes + 1] = joined[far, pl.ds(start, chans)]


def band_kernel(chans, height, dec, after, out):
    eye = (iota((chans, chans), 0) == iota((chans, chans), 1)).astype(F32).astype(BF16)
    step = 3 * chans
    wide = out.shape[1]
    for c in range(3):
        taps = [dot_nt(eye, dec[:, b, c].reshape(step, chans)) for b in range(3)]
        base = jnp.concatenate(taps + [jnp.zeros((chans, wide - 3 * step), F32)], axis=1)
        for h in range(height):
            row = h * step + c * chans
            moved = base if h == 0 else pltpu.roll(base, h * step, 1)
            out[row : row + chans] = moved.astype(BF16)


def decode_pair(chans, height, band, planes, spread, store):
    step = 3 * chans
    blocks = [jnp.concatenate([plane(h) for plane in planes], axis=1) for h in range(height + 2)]
    window = jnp.concatenate(blocks, axis=0)
    width = window.shape[1] // 2
    sums = [None] * height
    for at in range(0, window.shape[0], 256):
        stop = min(at + 256, window.shape[0])
        first = max(0, at // step - 2)
        last = min(height - 1, (stop - 1) // step)
        part = dot(band[first * step : (last + 1) * step, at:stop], window[at:stop])
        for h in range(first, last + 1):
            piece = part[(h - first) * step : (h - first + 1) * step]
            sums[h] = piece if sums[h] is None else sums[h] + piece
    lane = iota((chans, width), 1)
    for e in range(2):
        for h in range(height):
            part = sums[h][:, e * width : (e + 1) * width]
            before = jnp.where(lane == 0, 0.0, pltpu.roll(part[:chans], 1, 1))
            after = jnp.where(lane == width - 1, 0.0, pltpu.roll(part[2 * chans :], width - 1, 1))
            spread[e, pl.ds(h, chans, stride=height), :] = silu(part[chans : 2 * chans] + before + after)
        store(e, spread[e].astype(BF16))


def fill(field, slot, chans, plane, borders):
    height = field.shape[0]
    at = slice(slot * chans, (slot + 1) * chans)
    for h in range(1, height - 1):
        field[h, at] = plane[(h - 1) * chans : h * chans]
    if len(borders) == 1:
        col = lax.axis_index("col")
        field[(height - 1) * col, at] = jnp.zeros_like(borders[0])
        field[(height - 1) * (1 - col), at] = borders[0]
    else:
        field[0, at] = borders[0]
        field[height - 1, at] = borders[1]


def interior_kernel(chans, height, band, joined, *rest):
    sides, (out_hbm, field, spread, held, sems) = rest[:-5], rest[-5:]
    planes = joined.shape[0]
    for d in range(planes):
        fill(field, d, chans, joined[d], [side[d] for side in sides])
    copies = []
    for step in range(planes // 2 - 1):
        views = [
            lambda h, at=(2 * step + e) * chans: field[h, at : at + 3 * chans] for e in range(2)
        ]

        def store(e, value):
            held[2 * step + e] = value

        decode_pair(chans, height, band, views, spread.at[step], store)
        copies.append(
            pltpu.make_async_copy(
                held.at[2 * step : 2 * step + 2], out_hbm.at[2 * step + 1 : 2 * step + 3], sems.at[step]
            )
        )
        copies[-1].start()
    for copy in copies:
        copy.wait()


def edge_kernel(chans, height, band, joined, near, far, *rest):
    sides, (mid_hbm, out_hbm, field, spread, held, sems) = rest[:-6], rest[-6:]
    planes, rows, width = joined.shape
    for slot, d in ((1, 0), (2, 1), (3, planes - 2), (4, planes - 1)):
        fill(field, slot, chans, joined[d], [side[d] for side in sides])
    row, last = lax.axis_index("row"), lax.axis_size("row") - 1

    def outer(slot, got):
        borders = [got[rows + k * chans : rows + (k + 1) * chans] for k in range(len(sides))]
        fill(field, slot, chans, got[:rows], borders)

    @pl.when(row % 2 == 0)
    def _():
        outer(0, far[...])
        outer(5, near[...])

    @pl.when(row % 2 == 1)
    def _():
        outer(0, near[...])
        outer(5, far[...])

    @pl.when(row == 0)
    def _():
        field[:, :chans] = jnp.zeros((height + 2, chans, width), BF16)

    @pl.when(row == last)
    def _():
        field[:, 5 * chans :] = jnp.zeros((height + 2, chans, width), BF16)

    copies = [
        pltpu.make_async_copy(held.at[e], out_hbm.at[d], sems.at[e]) for e, d in ((0, 0), (1, planes - 1))
    ]

    def store(e, value):
        held[e] = value
        copies[e].start()

    views = [lambda h, at=3 * e * chans: field[h, at : at + 3 * chans] for e in range(2)]
    decode_pair(chans, height, band, views, spread, store)
    for copy in copies:
        copy.wait()


VMEM = pl.BlockSpec(memory_space=pltpu.MemorySpace.VMEM)
HBM = pl.BlockSpec(memory_space=pltpu.MemorySpace.HBM)


def fixed(x):
    return pltpu.with_memory_space_constraint(x, pltpu.MemorySpace.HBM)


def call(kernel, name, shape, ins, out, scratch=(), aliases=None, cost=0, limit=24):
    return pl.pallas_call(
        kernel,
        out_shape=shape,
        in_specs=ins,
        out_specs=out,
        scratch_shapes=list(scratch),
        input_output_aliases=aliases or {},
        name=name,
        cost_estimate=pl.CostEstimate(flops=cost, bytes_accessed=cost // 100, transcendentals=0),
        compiler_params=pltpu.CompilerParams(vmem_limit_bytes=limit << 20),
    )


def bf16(*shape):
    return jax.ShapeDtypeStruct(shape, BF16)


def neighbour_swaps(count, cols):
    ids = lambda row, col: row * cols + col
    first = [(ids(r, c), ids(r ^ 1, c)) for r in range(count) for c in range(cols)]
    second = []
    for r in range(count):
        for c in range(cols):
            other = r + 1 if r % 2 else r - 1
            inside = 0 <= other < count
            second.append((ids(r, c), ids(other, c) if inside else ids(r, c ^ 1)))
    return first, second


def body(features, down_weight, bott_weight, up_weight, dec_weight):
    depth, chans, height, width = features.shape
    count, cols = lax.axis_size("row"), lax.axis_size("col")
    top = down_weight.shape[4]
    coarse, rows, each = width // 8, chans * height, bott_weight.shape[3]
    feat = features.reshape(depth, rows, width)

    sems = lambda n: pltpu.SemaphoreType.DMA((n,))
    scratch = [pltpu.VMEM(feat.shape, BF16), pltpu.VMEM(down_weight.shape, BF16)]
    up_one = [(i, i + 1) for i in range(cols - 1)]
    down_one = [(i + 1, i) for i in range(cols - 1)]
    if cols == 2:
        size = top // 4
        held = bf16(3, 3, 3, each, size)
        lowered, keep, give = call(
            functools.partial(lower_pair_kernel, count, chans, height),
            "lower",
            (bf16(2 * count, coarse // 2, 4 * each), held, held),
            [HBM] * 3,
            (VMEM,) * 3,
            scratch + [sems(depth + 2)],
            cost=1_000_000_000,
        )(fixed(feat), fixed(down_weight), fixed(bott_weight))
        took = lax.ppermute(give, "row", [(i, i ^ 1) for i in range(count)])
        got = lax.all_to_all(lowered, ("row", "col"), split_axis=0, concat_axis=0, tiled=True)
        shares = call(
            bottleneck_pair_kernel,
            "bottleneck",
            bf16(2 * count, coarse, size),
            [VMEM] * 3,
            VMEM,
            [pltpu.VMEM(((count + 2) * coarse, 12 * each), BF16)],
            cost=2_000_000_000,
        )(got.reshape(count, 2, coarse // 2, 4 * each), keep, took)
        parts = lax.all_to_all(shares, ("row", "col"), split_axis=0, concat_axis=0, tiled=True)
    else:
        lowered = call(
            functools.partial(lower_kernel, count, chans, height),
            "lower",
            bf16(count, coarse, 3 * each),
            [HBM] * 2,
            VMEM,
            scratch + [sems(depth)],
            cost=1_000_000_000,
        )(fixed(feat), fixed(down_weight))
        own = lax.all_to_all(lowered, "row", split_axis=0, concat_axis=0, tiled=True)
        shares = call(
            bottleneck_kernel,
            "bottleneck",
            bf16(count, coarse, top),
            [VMEM] * 4,
            VMEM,
            [pltpu.VMEM(((count + 2) * coarse, 3 * each), BF16)] * 3,
            cost=2_000_000_000,
        )(lax.ppermute(own, "col", up_one), own, lax.ppermute(own, "col", down_one), bott_weight)
        parts = lax.all_to_all(shares, "row", split_axis=0, concat_axis=0, tiled=True)

    side = bf16(depth + 2, chans, width)
    sides = 1 if cols == 2 else 2
    joined, ends, *sides = call(
        functools.partial(raise_kernel, chans, height),
        "raise",
        (bf16(depth, rows, width), bf16(2, rows, width)) + (side,) * sides,
        [VMEM] * 3,
        (VMEM,) * (2 + sides),
        [pltpu.VMEM(feat.shape, F32)],
    )(parts, feat, up_weight)
    if cols == 2:
        sides = [lax.ppermute(sides[0], "col", up_one + down_one)]
    else:
        sides = [lax.ppermute(sides[1], "col", up_one), lax.ppermute(sides[0], "col", down_one)]

    span = rows + 2 * chans
    band = call(
        functools.partial(band_kernel, chans, height),
        "band",
        bf16(3 * rows, -(-3 * span // 128) * 128),
        [VMEM, HBM],
        VMEM,
        cost=500_000_000,
    )(dec_weight, joined)

    got = []
    for k, pairs in enumerate(neighbour_swaps(count, cols)):
        sent = jnp.concatenate([ends[k]] + [side[depth + k] for side in sides], axis=0)
        got.append(lax.ppermute(sent, ("row", "col"), pairs))

    shape = bf16(depth, rows, width)
    inner = call(
        functools.partial(interior_kernel, chans, height),
        "interior",
        shape,
        [VMEM] * (2 + len(sides)),
        HBM,
        [
            pltpu.VMEM((height + 2, depth * chans, width), BF16),
            pltpu.VMEM((depth // 2 - 1, 2, rows, width), F32),
            pltpu.VMEM((depth - 2, rows, width), BF16),
            sems(depth // 2 - 1),
        ],
        cost=3_000_000_000,
    )(band, joined, *sides)
    decoded = call(
        functools.partial(edge_kernel, chans, height),
        "edge",
        shape,
        [VMEM] * (4 + len(sides)) + [HBM],
        HBM,
        [
            pltpu.VMEM((height + 2, 6 * chans, width), BF16),
            pltpu.VMEM((2, rows, width), F32),
            pltpu.VMEM((2, rows, width), BF16),
            sems(2),
        ],
        aliases={4 + len(sides): 0},
        cost=1_000_000_000,
    )(band, joined, *got, *sides, inner)
    return decoded.reshape(depth, chans, height, width)


def solution(mesh):
    placed = (P("row", None, "col", None), P(), P(None, None, None, "row", None), P(), P())
    return jax.shard_map(
        body, mesh=mesh, in_specs=placed, out_specs=P("row", None, "col", None), check_vma=False
    )
```

```python
import functools

import jax
import jax.numpy as jnp
from jax import lax
from jax.experimental import pallas as pl
from jax.experimental.pallas import tpu as pltpu
from jax.sharding import PartitionSpec as P


F32, BF16 = jnp.float32, jnp.bfloat16
NT = (((1,), (1,)), ((), ()))


def iota(shape, dim):
    return lax.broadcasted_iota(jnp.int32, shape, dim)


def dot(a, b):
    return jnp.dot(a, b, preferred_element_type=F32)


def dot_nt(a, b):
    return lax.dot_general(a, b, NT, preferred_element_type=F32)


def silu(v):
    half = 0.5 * v
    return half + half * jnp.tanh(half)


def lowered_rows(height, chans, loads, feat, down):
    planes, rows, width = feat.shape
    quarters = planes // 2
    coarse = width // 8
    top = down.shape[4]
    shape = (height // 2 * chans, rows)
    r, c = iota(shape, 0), iota(shape, 1)
    pick = ((r % chans == c // height) & (r // chans == (c % height) // 2)).astype(F32).astype(BF16)
    shape = (4 * coarse, width)
    r, c = iota(shape, 0), iota(shape, 1)
    cols = ((r % coarse == c // 8) & (r // coarse == (c % 8) // 2)).astype(F32).astype(BF16)
    for a in range(quarters):
        loads[a].wait()
    tables = [(dot(pick, feat[2 * a]) + dot(pick, feat[2 * a + 1])).astype(BF16) for a in range(quarters)]
    pooled = [(dot_nt(cols, table) * 0.125).astype(BF16) for table in tables]
    low = jnp.zeros((coarse, top), F32)
    for a in range(quarters):
        loads[quarters + a].wait()
        for c in range(4):
            low = low + dot(pooled[a][c * coarse : (c + 1) * coarse], down[a, :, c].reshape(-1, top))
    return silu(low)


def input_loads(feat_hbm, down_hbm, feat, down, sems):
    quarters = feat.shape[0] // 2
    return [
        pltpu.make_async_copy(feat_hbm.at[2 * a : 2 * a + 2], feat.at[2 * a : 2 * a + 2], sems.at[a])
        for a in range(quarters)
    ] + [
        pltpu.make_async_copy(down_hbm.at[a], down.at[a], sems.at[quarters + a]) for a in range(quarters)
    ]


def lower_kernel(count, chans, height, feat_hbm, down_hbm, out, feat, down, sems):
    loads = input_loads(feat_hbm, down_hbm, feat, down, sems)
    for load in loads:
        load.start()
    low = lowered_rows(height, chans, loads, feat, down)
    coarse = low.shape[0]
    each = low.shape[1] // count
    place = iota(low.shape, 0)
    before = jnp.where(place == 0, 0.0, pltpu.roll(low, 1, 0))
    after = jnp.where(place == coarse - 1, 0.0, pltpu.roll(low, coarse - 1, 0))
    for k in range(count):
        part = slice(k * each, (k + 1) * each)
        out[k] = jnp.concatenate([before[:, part], low[:, part], after[:, part]], axis=1).astype(BF16)


def quarter(row, col, size):
    return pl.multiple_of((2 * (row % 2) + col) * size, size)


def lower_pair_kernel(count, chans, height, feat_hbm, down_hbm, bott_hbm, out, keep, give, feat, down, sems):
    loads = input_loads(feat_hbm, down_hbm, feat, down, sems)
    row, col = lax.axis_index("row"), lax.axis_index("col")
    taps, size = keep.shape
    edge = (feat.shape[0] - 1) * (1 - row % 2)
    quarters = [
        pltpu.make_async_copy(
            bott_hbm.at[:, pl.ds(quarter(row + 1, col, size), size)], give.at[:taps], sems.at[len(loads)]
        ),
        pltpu.make_async_copy(feat_hbm.at[edge], give.at[taps:], sems.at[len(loads) + 1]),
        pltpu.make_async_copy(
            bott_hbm.at[:, pl.ds(quarter(row, col, size), size)], keep, sems.at[len(loads) + 2]
        ),
    ]
    for load in loads + quarters:
        load.start()
    low = lowered_rows(height, chans, loads, feat, down)
    half = low.shape[0] // 2
    each = low.shape[1] // count
    for k in range(count):
        pieces = []
        for rows in (slice(0, half), slice(half, 2 * half)):
            for owner in (k, k ^ 1):
                pieces.append(low[rows, owner * each : (owner + 1) * each])
        block = jnp.concatenate(pieces, axis=1).astype(BF16)
        out[2 * k] = block
        out[2 * k + 1] = block
    for load in quarters:
        load.wait()


def bottleneck_kernel(*refs):
    blocks, weight, out, pads = refs[:3], refs[3], refs[4], refs[5:]
    depth, coarse, top = out.shape
    rows = depth * coarse
    lanes = 3 * weight.shape[3]
    total = jnp.zeros((rows, top), F32)
    for tap, (block, pad) in enumerate(zip(blocks, pads)):
        zero = jnp.zeros((coarse, lanes), BF16)
        pad[:coarse] = zero
        pad[coarse + rows :] = zero
        pad[coarse : coarse + rows] = block[...].reshape(rows, lanes)
        for a in range(3):
            kernel = weight[a, tap].reshape(lanes, top)
            total = total + dot(pad[a * coarse : a * coarse + rows], kernel)
    out[...] = total.astype(BF16).reshape(out.shape)


def bottleneck_pair_kernel(got, keep, took, out, pad):
    depth, _, half, lanes = got.shape
    group = lanes // 2
    coarse = 2 * half
    rows = depth * coarse
    each = group // 2
    lane = iota((half, lanes), 1)
    blocks = []
    for d in range(depth):
        low, high = got[d, 0].astype(F32), got[d, 1].astype(F32)
        blocks.append(jnp.where(lane < group, low, pltpu.roll(high, group, 1)))
        blocks.append(jnp.where(lane < group, pltpu.roll(low, group, 1), high))
    here = jnp.concatenate(blocks, axis=0)
    place = iota((rows, lanes), 0) % coarse
    before = jnp.where(place == 0, 0.0, pltpu.roll(here, 1, 0))
    after = jnp.where(place == coarse - 1, 0.0, pltpu.roll(here, rows - 1, 0))
    zero = jnp.zeros((coarse, 3 * lanes), BF16)
    pad[:coarse] = zero
    pad[coarse + rows :] = zero
    for c, value in enumerate((before, here, after)):
        pad[coarse : coarse + rows, c * lanes : (c + 1) * lanes] = value.astype(BF16)
    total = None
    for a in range(3):
        bands = []
        for c in range(3):
            for source in range(2):
                for held in (keep, took):
                    at = [((3 * a + source - h + 1) * 3 + c) * each for h in range(2)]
                    bands.append(jnp.concatenate([held[k : k + each] for k in at], axis=1))
        term = dot(pad[a * coarse : a * coarse + rows], jnp.concatenate(bands, axis=0))
        total = term if total is None else total + term
    size = out.shape[2]
    for h in range(2):
        for d in range(depth):
            out[2 * d + h] = total[d * coarse : (d + 1) * coarse, h * size : (h + 1) * size].astype(BF16)


def raise_kernel(chans, height, parts, feat, up, joined, first, second, *rest):
    sides, spread = rest[:-1], rest[-1]
    planes, rows, width = feat.shape
    coarse = width // 8
    groups = up.shape[4] // parts.shape[2]
    sums = []
    for q in range(groups):
        total = parts[q].astype(F32)
        for k in range(q + groups, parts.shape[0], groups):
            total = total + parts[k].astype(F32)
        sums.append(total)
    middle = silu(sums[0] if groups == 1 else jnp.concatenate(sums, axis=1)).astype(BF16)
    shape = (4 * width, coarse)
    r, c = iota(shape, 0), iota(shape, 1)
    pick = (((r % width) // 8 == c) & ((r % 8) // 2 == r // width)).astype(F32).astype(BF16)
    wide = dot(pick, middle).astype(BF16)
    raised = None
    for c in range(4):
        weight = up[:, :, c].reshape(-1, up.shape[4])
        term = dot_nt(weight, wide[c * width : (c + 1) * width])
        raised = term if raised is None else raised + term
    per = chans * (height // 2)
    for d in range(planes):
        spread[d] = feat[d].astype(F32)
        for h in range(height):
            start = (d // 2) * per + (h // 2) * chans
            value = spread[d, pl.ds(h, chans, stride=height), :] + raised[start : start + chans]
            joined[d, h * chans : (h + 1) * chans] = value.astype(BF16)
    odd = lax.axis_index("row") % 2
    near, far = (planes - 1) * (1 - odd), (planes - 1) * odd
    if first.shape[0] == rows:
        first[...] = joined[near]
    else:
        first[...] = jnp.where(odd == 1, raised[:per], raised[-per:]).astype(BF16)
    second[...] = joined[far]
    if len(sides) == 1:
        starts = [pl.multiple_of((rows - chans) * (1 - lax.axis_index("col")), chans)]
    else:
        starts = [0, rows - chans]
    for side, start in zip(sides, starts):
        for d in range(planes):
            side[d] = joined[d, pl.ds(start, chans)]
        side[planes] = joined[near, pl.ds(start, chans)]
        side[planes + 1] = joined[far, pl.ds(start, chans)]


def band_kernel(chans, height, dec, after, out):
    eye = (iota((chans, chans), 0) == iota((chans, chans), 1)).astype(F32).astype(BF16)
    step = 3 * chans
    wide = out.shape[1]
    for c in range(3):
        taps = [dot_nt(eye, dec[:, b, c].reshape(step, chans)) for b in range(3)]
        base = jnp.concatenate(taps + [jnp.zeros((chans, wide - 3 * step), F32)], axis=1)
        for h in range(height):
            row = h * step + c * chans
            moved = base if h == 0 else pltpu.roll(base, h * step, 1)
            out[row : row + chans] = moved.astype(BF16)


def decode_pair(chans, height, band, planes, spread, store):
    step = 3 * chans
    blocks = [jnp.concatenate([plane(h) for plane in planes], axis=1) for h in range(height + 2)]
    window = jnp.concatenate(blocks, axis=0)
    width = window.shape[1] // 2
    sums = [None] * height
    for at in range(0, window.shape[0], 256):
        stop = min(at + 256, window.shape[0])
        first = max(0, at // step - 2)
        last = min(height - 1, (stop - 1) // step)
        part = dot(band[first * step : (last + 1) * step, at:stop], window[at:stop])
        for h in range(first, last + 1):
            piece = part[(h - first) * step : (h - first + 1) * step]
            sums[h] = piece if sums[h] is None else sums[h] + piece
    lane = iota((chans, width), 1)
    for e in range(2):
        for h in range(height):
            part = sums[h][:, e * width : (e + 1) * width]
            before = jnp.where(lane == 0, 0.0, pltpu.roll(part[:chans], 1, 1))
            after = jnp.where(lane == width - 1, 0.0, pltpu.roll(part[2 * chans :], width - 1, 1))
            spread[e, pl.ds(h, chans, stride=height), :] = silu(part[chans : 2 * chans] + before + after)
        store(e, spread[e].astype(BF16))


def fill(field, slot, chans, plane, borders):
    height = field.shape[0]
    at = slice(slot * chans, (slot + 1) * chans)
    for h in range(1, height - 1):
        field[h, at] = plane[(h - 1) * chans : h * chans]
    if len(borders) == 1:
        col = lax.axis_index("col")
        field[(height - 1) * col, at] = jnp.zeros_like(borders[0])
        field[(height - 1) * (1 - col), at] = borders[0]
    else:
        field[0, at] = borders[0]
        field[height - 1, at] = borders[1]


def interior_kernel(chans, height, band, joined, *rest):
    sides, (out_hbm, field, spread, held, sems) = rest[:-5], rest[-5:]
    planes = joined.shape[0]
    for d in range(planes):
        fill(field, d, chans, joined[d], [side[d] for side in sides])
    copies = []
    for step in range(planes // 2 - 1):
        views = [
            lambda h, at=(2 * step + e) * chans: field[h, at : at + 3 * chans] for e in range(2)
        ]

        def store(e, value):
            held[2 * step + e] = value

        decode_pair(chans, height, band, views, spread.at[step], store)
        copies.append(
            pltpu.make_async_copy(
                held.at[2 * step : 2 * step + 2], out_hbm.at[2 * step + 1 : 2 * step + 3], sems.at[step]
            )
        )
        copies[-1].start()
    for copy in copies:
        copy.wait()


def nearby_kernel(chans, height, took, near, plane, corner, spread):
    rows = plane.shape[0]
    spread[...] = took[-rows:].astype(F32)
    for h in range(height):
        at = (h // 2) * chans
        value = spread[pl.ds(h, chans, stride=height), :] + near[at : at + chans].astype(F32)
        plane[h * chans : (h + 1) * chans] = value.astype(BF16)
    corner[...] = plane[pl.ds(pl.multiple_of((rows - chans) * (1 - lax.axis_index("col")), chans), chans)]


def edge_kernel(chans, height, band, joined, near, near_rows, far, far_rows, *rest):
    sides, (mid_hbm, out_hbm, field, spread, held, sems) = rest[:-6], rest[-6:]
    planes, _, width = joined.shape
    for slot, d in ((1, 0), (2, 1), (3, planes - 2), (4, planes - 1)):
        fill(field, slot, chans, joined[d], [side[d] for side in sides])
    row, last = lax.axis_index("row"), lax.axis_size("row") - 1

    def outer(slot, plane, corners):
        fill(field, slot, chans, plane[...], [corners[k * chans : (k + 1) * chans] for k in range(len(sides))])

    @pl.when(row % 2 == 0)
    def _():
        outer(0, far, far_rows)
        outer(5, near, near_rows)

    @pl.when(row % 2 == 1)
    def _():
        outer(0, near, near_rows)
        outer(5, far, far_rows)

    @pl.when(row == 0)
    def _():
        field[:, :chans] = jnp.zeros((height + 2, chans, width), BF16)

    @pl.when(row == last)
    def _():
        field[:, 5 * chans :] = jnp.zeros((height + 2, chans, width), BF16)

    copies = [
        pltpu.make_async_copy(held.at[e], out_hbm.at[d], sems.at[e]) for e, d in ((0, 0), (1, planes - 1))
    ]

    def store(e, value):
        held[e] = value
        copies[e].start()

    views = [lambda h, at=3 * e * chans: field[h, at : at + 3 * chans] for e in range(2)]
    decode_pair(chans, height, band, views, spread, store)
    for copy in copies:
        copy.wait()


VMEM = pl.BlockSpec(memory_space=pltpu.MemorySpace.VMEM)
HBM = pl.BlockSpec(memory_space=pltpu.MemorySpace.HBM)


def fixed(x):
    return pltpu.with_memory_space_constraint(x, pltpu.MemorySpace.HBM)


def call(kernel, shape, ins, out, scratch=(), aliases=None, cost=0, limit=24):
    return pl.pallas_call(
        kernel,
        out_shape=shape,
        in_specs=ins,
        out_specs=out,
        scratch_shapes=list(scratch),
        input_output_aliases=aliases or {},
        cost_estimate=pl.CostEstimate(flops=cost, bytes_accessed=cost // 100, transcendentals=0),
        compiler_params=pltpu.CompilerParams(vmem_limit_bytes=limit << 20),
    )


def bf16(*shape):
    return jax.ShapeDtypeStruct(shape, BF16)


def neighbour_swaps(count, cols):
    ids = lambda row, col: row * cols + col
    first = [(ids(r, c), ids(r ^ 1, c)) for r in range(count) for c in range(cols)]
    second = []
    for r in range(count):
        for c in range(cols):
            other = r + 1 if r % 2 else r - 1
            inside = 0 <= other < count
            second.append((ids(r, c), ids(other, c) if inside else ids(r, c ^ 1)))
    return first, second


def level(features, down_weight, bott_weight, up_weight, dec_weight):
    depth, chans, height, width = features.shape
    count, cols = lax.axis_size("row"), lax.axis_size("col")
    top = down_weight.shape[4]
    coarse, rows, each = width // 8, chans * height, bott_weight.shape[3]
    feat = features.reshape(depth, rows, width)

    sems = lambda n: pltpu.SemaphoreType.DMA((n,))
    scratch = [pltpu.VMEM(feat.shape, BF16), pltpu.VMEM(down_weight.shape, BF16)]
    up_one = [(i, i + 1) for i in range(cols - 1)]
    down_one = [(i + 1, i) for i in range(cols - 1)]
    paired = cols == 2 and top // 4 == width
    if paired:
        size = top // 4
        taps = bott_weight.shape[0] * bott_weight.shape[1] * bott_weight.shape[2] * each
        lowered, keep, give = call(
            functools.partial(lower_pair_kernel, count, chans, height),
            (bf16(2 * count, coarse // 2, 4 * each), bf16(taps, size), bf16(taps + rows, size)),
            [HBM] * 3,
            (VMEM,) * 3,
            scratch + [sems(depth + 3)],
            cost=1_000_000_000,
        )(fixed(feat), fixed(down_weight), fixed(bott_weight.reshape(taps, top)))
        took = lax.ppermute(give, "row", [(i, i ^ 1) for i in range(count)])
        got = lax.all_to_all(lowered, ("row", "col"), split_axis=0, concat_axis=0, tiled=True)
        shares = call(
            bottleneck_pair_kernel,
            bf16(2 * count, coarse, size),
            [VMEM] * 3,
            VMEM,
            [pltpu.VMEM(((count + 2) * coarse, 12 * each), BF16)],
            cost=2_000_000_000,
        )(got.reshape(count, 2, coarse // 2, 4 * each), keep, took)
        parts = lax.all_to_all(shares, ("row", "col"), split_axis=0, concat_axis=0, tiled=True)
    else:
        lowered = call(
            functools.partial(lower_kernel, count, chans, height),
            bf16(count, coarse, 3 * each),
            [HBM] * 2,
            VMEM,
            scratch + [sems(depth)],
            cost=1_000_000_000,
        )(fixed(feat), fixed(down_weight))
        own = lax.all_to_all(lowered, "row", split_axis=0, concat_axis=0, tiled=True)
        shares = call(
            bottleneck_kernel,
            bf16(count, coarse, top),
            [VMEM] * 4,
            VMEM,
            [pltpu.VMEM(((count + 2) * coarse, 3 * each), BF16)] * 3,
            cost=2_000_000_000,
        )(lax.ppermute(own, "col", up_one), own, lax.ppermute(own, "col", down_one), bott_weight)
        parts = lax.all_to_all(shares, "row", split_axis=0, concat_axis=0, tiled=True)

    side = bf16(depth + 2, chans, width)
    sides = 1 if cols == 2 else 2
    joined, *ends = call(
        functools.partial(raise_kernel, chans, height),
        (bf16(depth, rows, width), bf16(rows // 2 if paired else rows, width), bf16(rows, width)) + (side,) * sides,
        [VMEM] * 3,
        (VMEM,) * (3 + sides),
        [pltpu.VMEM(feat.shape, F32)],
    )(parts, feat, up_weight)
    ends, sides = ends[:2], ends[2:]
    if cols == 2:
        sides = [lax.ppermute(sides[0], "col", up_one + down_one)]
    else:
        sides = [lax.ppermute(sides[1], "col", up_one), lax.ppermute(sides[0], "col", down_one)]

    span = rows + 2 * chans
    band = call(
        functools.partial(band_kernel, chans, height),
        bf16(3 * rows, -(-3 * span // 128) * 128),
        [VMEM, HBM],
        VMEM,
        cost=500_000_000,
    )(dec_weight, joined)

    got = []
    for k, pairs in enumerate(neighbour_swaps(count, cols)):
        alone = paired and k == 0
        sent = ends[k] if alone else jnp.concatenate([ends[k]] + [side[depth + k] for side in sides], axis=0)
        swapped = lax.ppermute(sent, ("row", "col"), pairs)
        if alone:
            plane, corner = call(
                functools.partial(nearby_kernel, chans, height),
                (bf16(rows, width), bf16(chans, width)),
                [VMEM] * 2,
                (VMEM,) * 2,
                [pltpu.VMEM((rows, width), F32)],
            )(took, swapped)
            got += [plane, lax.ppermute(corner, "col", up_one + down_one)]
        else:
            got += [swapped[:rows], swapped[rows:]]

    shape = bf16(depth, rows, width)
    inner = call(
        functools.partial(interior_kernel, chans, height),
        shape,
        [VMEM] * (2 + len(sides)),
        HBM,
        [
            pltpu.VMEM((height + 2, depth * chans, width), BF16),
            pltpu.VMEM((depth // 2 - 1, 2, rows, width), F32),
            pltpu.VMEM((depth - 2, rows, width), BF16),
            sems(depth // 2 - 1),
        ],
        cost=3_000_000_000,
    )(band, joined, *sides)
    decoded = call(
        functools.partial(edge_kernel, chans, height),
        shape,
        [VMEM] * (6 + len(sides)) + [HBM],
        HBM,
        [
            pltpu.VMEM((height + 2, 6 * chans, width), BF16),
            pltpu.VMEM((2, rows, width), F32),
            pltpu.VMEM((2, rows, width), BF16),
            sems(2),
        ],
        aliases={6 + len(sides): 0},
        cost=1_000_000_000,
    )(band, joined, *got, *sides, inner)
    return decoded.reshape(depth, chans, height, width)


def solution(mesh):
    placed = (P("row", None, "col", None), P(), P(None, None, None, "row", None), P(), P())
    return jax.shard_map(level, mesh=mesh, in_specs=placed, out_specs=P("row", None, "col", None), check_vma=False)
```

```python
import functools

import jax
import jax.numpy as jnp
from jax import lax
from jax.experimental import pallas as pl
from jax.experimental.pallas import tpu as pltpu
from jax.sharding import PartitionSpec as P


F32, BF16 = jnp.float32, jnp.bfloat16
NT = (((1,), (1,)), ((), ()))


def iota(shape, dim):
    return lax.broadcasted_iota(jnp.int32, shape, dim)


def dot(a, b):
    return jnp.dot(a, b, preferred_element_type=F32)


def dot_nt(a, b):
    return lax.dot_general(a, b, NT, preferred_element_type=F32)


def silu(v):
    half = 0.5 * v
    return half + half * jnp.tanh(half)


def lowered_rows(height, chans, loads, feat, down):
    planes, rows, width = feat.shape
    quarters = planes // 2
    coarse = width // 8
    top = down.shape[4]
    shape = (height // 2 * chans, rows)
    r, c = iota(shape, 0), iota(shape, 1)
    pick = ((r % chans == c // height) & (r // chans == (c % height) // 2)).astype(F32).astype(BF16)
    shape = (4 * coarse, width)
    r, c = iota(shape, 0), iota(shape, 1)
    cols = ((r % coarse == c // 8) & (r // coarse == (c % 8) // 2)).astype(F32).astype(BF16)
    loads[0].wait()
    tables = [(dot(pick, feat[2 * a]) + dot(pick, feat[2 * a + 1])).astype(BF16) for a in range(quarters)]
    pooled = [(dot_nt(cols, table) * 0.125).astype(BF16) for table in tables]
    low = jnp.zeros((coarse, top), F32)
    for a in range(quarters):
        for load in loads[1 + 2 * a : 3 + 2 * a]:
            load.wait()
        for c in range(4):
            low = low + dot(pooled[a][c * coarse : (c + 1) * coarse], down[a, :, c].reshape(-1, top))
    return silu(low)


def input_loads(feat_hbm, down_hbm, feat, down, sems):
    taps, half = down.shape[0], down.shape[1] // 2
    loads = [pltpu.make_async_copy(feat_hbm, feat, sems.at[0])]
    for a in range(taps):
        for part in (slice(0, half), slice(half, 2 * half)):
            loads.append(pltpu.make_async_copy(down_hbm.at[a, part], down.at[a, part], sems.at[len(loads)]))
    return loads


def lower_kernel(count, chans, height, feat_hbm, down_hbm, out, feat, down, sems):
    loads = input_loads(feat_hbm, down_hbm, feat, down, sems)
    for load in loads:
        load.start()
    low = lowered_rows(height, chans, loads, feat, down)
    coarse = low.shape[0]
    each = low.shape[1] // count
    place = iota(low.shape, 0)
    before = jnp.where(place == 0, 0.0, pltpu.roll(low, 1, 0))
    after = jnp.where(place == coarse - 1, 0.0, pltpu.roll(low, coarse - 1, 0))
    for k in range(count):
        part = slice(k * each, (k + 1) * each)
        out[k] = jnp.concatenate([before[:, part], low[:, part], after[:, part]], axis=1).astype(BF16)


def quarter(row, col, size):
    return pl.multiple_of((2 * (row % 2) + col) * size, size)


def lower_pair_kernel(count, chans, height, feat_hbm, down_hbm, bott_hbm, out, keep, give, feat, down, sems):
    loads = input_loads(feat_hbm, down_hbm, feat, down, sems)
    row, col = lax.axis_index("row"), lax.axis_index("col")
    taps, size = keep.shape
    edge = (feat.shape[0] - 1) * (1 - row % 2)
    quarters = [
        pltpu.make_async_copy(
            bott_hbm.at[:, pl.ds(quarter(row + 1, col, size), size)], give.at[:taps], sems.at[len(loads)]
        ),
        pltpu.make_async_copy(feat_hbm.at[edge], give.at[taps:], sems.at[len(loads) + 1]),
        pltpu.make_async_copy(
            bott_hbm.at[:, pl.ds(quarter(row, col, size), size)], keep, sems.at[len(loads) + 2]
        ),
    ]
    for load in loads + quarters:
        load.start()
    low = lowered_rows(height, chans, loads, feat, down)
    half = low.shape[0] // 2
    each = low.shape[1] // count
    for k in range(count):
        pieces = []
        for rows in (slice(0, half), slice(half, 2 * half)):
            for owner in (k, k ^ 1):
                pieces.append(low[rows, owner * each : (owner + 1) * each])
        block = jnp.concatenate(pieces, axis=1).astype(BF16)
        out[2 * k] = block
        out[2 * k + 1] = block
    for load in quarters:
        load.wait()


def bottleneck_kernel(*refs):
    blocks, weight, out, pads = refs[:3], refs[3], refs[4], refs[5:]
    depth, coarse, top = out.shape
    rows = depth * coarse
    lanes = 3 * weight.shape[3]
    total = jnp.zeros((rows, top), F32)
    for tap, (block, pad) in enumerate(zip(blocks, pads)):
        zero = jnp.zeros((coarse, lanes), BF16)
        pad[:coarse] = zero
        pad[coarse + rows :] = zero
        pad[coarse : coarse + rows] = block[...].reshape(rows, lanes)
        for a in range(3):
            kernel = weight[a, tap].reshape(lanes, top)
            total = total + dot(pad[a * coarse : a * coarse + rows], kernel)
    out[...] = total.astype(BF16).reshape(out.shape)


def bottleneck_pair_kernel(got, keep, took, out, pad):
    depth, _, half, lanes = got.shape
    group = lanes // 2
    coarse = 2 * half
    rows = depth * coarse
    each = group // 2
    lane = iota((half, lanes), 1)
    blocks = []
    for d in range(depth):
        low, high = got[d, 0].astype(F32), got[d, 1].astype(F32)
        blocks.append(jnp.where(lane < group, low, pltpu.roll(high, group, 1)))
        blocks.append(jnp.where(lane < group, pltpu.roll(low, group, 1), high))
    here = jnp.concatenate(blocks, axis=0)
    place = iota((rows, lanes), 0) % coarse
    before = jnp.where(place == 0, 0.0, pltpu.roll(here, 1, 0))
    after = jnp.where(place == coarse - 1, 0.0, pltpu.roll(here, rows - 1, 0))
    zero = jnp.zeros((coarse, 3 * lanes), BF16)
    pad[:coarse] = zero
    pad[coarse + rows :] = zero
    for c, value in enumerate((before, here, after)):
        pad[coarse : coarse + rows, c * lanes : (c + 1) * lanes] = value.astype(BF16)
    total = None
    for a in range(3):
        bands = []
        for c in range(3):
            for source in range(2):
                for held in (keep, took):
                    at = [((3 * a + source - h + 1) * 3 + c) * each for h in range(2)]
                    bands.append(jnp.concatenate([held[k : k + each] for k in at], axis=1))
        term = dot(pad[a * coarse : a * coarse + rows], jnp.concatenate(bands, axis=0))
        total = term if total is None else total + term
    size = out.shape[2]
    for h in range(2):
        for d in range(depth):
            out[2 * d + h] = total[d * coarse : (d + 1) * coarse, h * size : (h + 1) * size].astype(BF16)


def join(chans, height, plane, raised, spread, store):
    spread[...] = plane.astype(F32)
    for h in range(height):
        at = (h // 2) * chans
        value = spread[pl.ds(h, chans, stride=height), :] + raised[at : at + chans].astype(F32)
        store(h * chans, value.astype(BF16))


def outer_kernel(chans, height, parts, feat, up, wide, first, second, spread):
    planes, rows, width = feat.shape
    coarse, top = width // 8, up.shape[4]
    groups = top // parts.shape[2]
    sums = []
    for q in range(groups):
        total = parts[q].astype(F32)
        for k in range(q + groups, parts.shape[0], groups):
            total = total + parts[k].astype(F32)
        sums.append(total)
    middle = silu(sums[0] if groups == 1 else jnp.concatenate(sums, axis=1))
    spreading = jnp.concatenate([jnp.broadcast_to(middle[w : w + 1], (8, top)) for w in range(coarse)], axis=0)
    which = iota(spreading.shape, 0) % 8 // 2
    odd = lax.axis_index("row") % 2
    last = up.shape[0] - 1
    steps = (last * (1 - odd), last * odd)
    raised = None
    for c in range(4):
        columns = jnp.where(which == c, spreading, 0.0).astype(BF16)
        wide[c * width : (c + 1) * width] = columns
        weight = jnp.concatenate([up[a, :, c].reshape(-1, top) for a in steps], axis=0)
        term = dot_nt(weight, columns)
        raised = term if raised is None else raised + term
    per = raised.shape[0] // 2

    def put(target):
        def store(at, value):
            target[at : at + chans] = value

        return store

    if first.shape[0] == rows:
        join(chans, height, feat[(planes - 1) * (1 - odd)], raised[:per], spread.at[0], put(first))
    else:
        first[...] = raised[:per].astype(BF16)
    join(chans, height, feat[(planes - 1) * odd], raised[per:], spread.at[1], put(second))


def raise_kernel(chans, height, wide, feat, up, joined, *rest):
    sides, spread = rest[:-1], rest[-1]
    planes, rows, width = feat.shape
    raised = None
    for c in range(4):
        weight = up[:, :, c].reshape(-1, up.shape[4])
        term = dot_nt(weight, wide[c * width : (c + 1) * width])
        raised = term if raised is None else raised + term
    per = chans * (height // 2)
    for d in range(planes):

        def store(at, value):
            joined[d, at : at + chans] = value

        join(chans, height, feat[d], raised[d // 2 * per : (d // 2 + 1) * per], spread.at[d], store)
    odd = lax.axis_index("row") % 2
    near, far = (planes - 1) * (1 - odd), (planes - 1) * odd
    if len(sides) == 1:
        starts = [pl.multiple_of((rows - chans) * (1 - lax.axis_index("col")), chans)]
    else:
        starts = [0, rows - chans]
    for side, start in zip(sides, starts):
        for d in range(planes):
            side[d] = joined[d, pl.ds(start, chans)]
        if side.shape[0] > planes:
            side[planes] = joined[near, pl.ds(start, chans)]
            side[planes + 1] = joined[far, pl.ds(start, chans)]


def band_kernel(chans, height, dec, after, out):
    eye = (iota((chans, chans), 0) == iota((chans, chans), 1)).astype(F32).astype(BF16)
    step = 3 * chans
    wide = out.shape[1]
    for c in range(3):
        taps = [dot_nt(eye, dec[:, b, c].reshape(step, chans)) for b in range(3)]
        base = jnp.concatenate(taps + [jnp.zeros((chans, wide - 3 * step), F32)], axis=1)
        for h in range(height):
            row = h * step + c * chans
            moved = base if h == 0 else pltpu.roll(base, h * step, 1)
            out[row : row + chans] = moved.astype(BF16)


def taps_of(chans, part):
    width = part.shape[1]
    lane = iota((chans, width), 1)
    before = jnp.where(lane == 0, 0.0, pltpu.roll(part[:chans], 1, 1))
    after = jnp.where(lane == width - 1, 0.0, pltpu.roll(part[2 * chans :], width - 1, 1))
    return silu(part[chans : 2 * chans] + before + after)


def decode_pair(chans, height, band, planes, spread, store):
    step = 3 * chans
    blocks = [jnp.concatenate([plane(h) for plane in planes], axis=1) for h in range(height + 2)]
    window = jnp.concatenate(blocks, axis=0)
    width = window.shape[1] // 2
    sums = [None] * height
    for at in range(0, window.shape[0], 256):
        stop = min(at + 256, window.shape[0])
        first = max(0, at // step - 2)
        last = min(height - 1, (stop - 1) // step)
        part = dot(band[first * step : (last + 1) * step, at:stop], window[at:stop])
        for h in range(first, last + 1):
            piece = part[(h - first) * step : (h - first + 1) * step]
            sums[h] = piece if sums[h] is None else sums[h] + piece
    for e in range(2):
        for h in range(height):
            value = taps_of(chans, sums[h][:, e * width : (e + 1) * width])
            spread[e, pl.ds(h, chans, stride=height), :] = value
        store(e)
    return sums


def fill(field, slot, chans, plane, borders):
    height = field.shape[0]
    at = slice(slot * chans, (slot + 1) * chans)
    for h in range(1, height - 1):
        field[h, at] = plane[(h - 1) * chans : h * chans]
    if len(borders) == 1:
        col = lax.axis_index("col")
        field[(height - 1) * col, at] = jnp.zeros_like(borders[0])
        field[(height - 1) * (1 - col), at] = borders[0]
    else:
        field[0, at] = borders[0]
        field[height - 1, at] = borders[1]


def interior_kernel(chans, height, band, joined, *rest):
    sides, (out, field, spread) = rest[:-3], rest[-3:]
    planes = joined.shape[0]
    for d in range(planes):
        fill(field, d, chans, joined[d], [side[d] for side in sides])
    for step in range(planes // 2 - 1):
        views = [lambda h, at=(2 * step + e) * chans: field[h, at : at + 3 * chans] for e in range(2)]

        def store(e):
            out[2 * step + e] = spread[step, e].astype(BF16)

        decode_pair(chans, height, band, views, spread.at[step], store)


def nearby_kernel(chans, height, took, near, far, plane, corners, spread):
    rows = plane.shape[0]

    def store(at, value):
        plane[at : at + chans] = value

    join(chans, height, took[-rows:], near, spread, store)
    start = pl.multiple_of((rows - chans) * (1 - lax.axis_index("col")), chans)
    corners[:chans] = plane[pl.ds(start, chans)]
    corners[chans:] = far[pl.ds(start, chans)]


def fill_edges(chans, joined, near, far, sides, near_rows, far_rows, field):
    planes, _, width = joined.shape
    for slot, d in ((1, 0), (2, 1), (3, planes - 2), (4, planes - 1)):
        fill(field, slot, chans, joined[d], [side[d] for side in sides])
    row, last = lax.axis_index("row"), lax.axis_size("row") - 1

    def outer(slot, plane, corners):
        fill(field, slot, chans, plane[...], corners)

    @pl.when(row % 2 == 0)
    def _():
        outer(0, far, far_rows)
        outer(5, near, near_rows)

    @pl.when(row % 2 == 1)
    def _():
        outer(0, near, near_rows)
        outer(5, far, far_rows)

    @pl.when(row == 0)
    def _():
        field[:, :chans] = jnp.zeros((field.shape[0], chans, width), BF16)

    @pl.when(row == last)
    def _():
        field[:, 5 * chans :] = jnp.zeros((field.shape[0], chans, width), BF16)


def edge_views(chans, field):
    return [lambda h, at=3 * e * chans: field[h, at : at + 3 * chans] for e in range(2)]


def result_copies(inner, held, out_hbm, sems):
    last = out_hbm.shape[0] - 1
    pieces = ((inner, out_hbm.at[1:last]), (held.at[0], out_hbm.at[0]), (held.at[1], out_hbm.at[last]))
    return [pltpu.make_async_copy(piece, place, sems.at[k]) for k, (piece, place) in enumerate(pieces)]


def edge_kernel(chans, height, band, joined, near, near_rows, far, far_rows, *rest):
    sides, (inner, out_hbm, field, spread, held, sems) = rest[:-6], rest[-6:]
    copies = result_copies(inner, held, out_hbm, sems)
    copies[0].start()
    borders = [[got[k * chans : (k + 1) * chans] for k in range(len(sides))] for got in (near_rows, far_rows)]
    fill_edges(chans, joined, near, far, sides, *borders, field)

    def store(e):
        held[e] = spread[e].astype(BF16)
        copies[1 + e].start()

    decode_pair(chans, height, band, edge_views(chans, field), spread, store)
    for copy in copies:
        copy.wait()


def early_edge_kernel(chans, height, band, joined, near, far, side, values, partial, field):
    none = [jnp.zeros((chans, joined.shape[2]), BF16)]
    fill_edges(chans, joined, near, far, [side], none, none, field)
    sums = decode_pair(chans, height, band, edge_views(chans, field), values, lambda e: None)
    partial[...] = jnp.where(lax.axis_index("col") == 0, sums[-1], sums[0])


def late_edge_kernel(chans, height, band, corners, values, partial, inner, out_hbm, window, spread, held, sems):
    copies = result_copies(inner, held, out_hbm, sems)
    copies[0].start()
    row, last, col = lax.axis_index("row"), lax.axis_size("row") - 1, lax.axis_index("col")
    step, width = 3 * chans, corners.shape[1]
    tile = window.shape[0]
    at_tile = pl.multiple_of((height + 2) * step // tile * tile * (1 - col), tile)
    at_row = (height + 1) * step % tile * (1 - col)
    window[...] = jnp.zeros(window.shape, BF16)

    def put(tap, got):
        window[pl.ds(pl.multiple_of(at_row + tap * chans, chans), chans), tap // 2 * width : (tap // 2 + 1) * width] = got

    even = row % 2 == 0

    @pl.when((row > 0) & even)
    def _():
        put(0, corners[chans:])

    @pl.when((row > 0) & ~even)
    def _():
        put(0, corners[:chans])

    @pl.when((row < last) & even)
    def _():
        put(2, corners[:chans])

    @pl.when((row < last) & ~even)
    def _():
        put(2, corners[chans:])

    edge = (height - 1) * (1 - col)
    kernel = band[pl.ds(pl.multiple_of(edge * step, step), step), pl.ds(at_tile, tile)]
    sums = partial[...] + dot(kernel, window[...])
    for e in range(2):
        spread[e] = values[e]
        spread[e, pl.ds(edge, chans, stride=height), :] = taps_of(chans, sums[:, e * width : (e + 1) * width])
        held[e] = spread[e].astype(BF16)
        copies[1 + e].start()
    for copy in copies:
        copy.wait()


VMEM = pl.BlockSpec(memory_space=pltpu.MemorySpace.VMEM)
HBM = pl.BlockSpec(memory_space=pltpu.MemorySpace.HBM)


def fixed(x):
    return pltpu.with_memory_space_constraint(x, pltpu.MemorySpace.HBM)


def call(kernel, shape, ins, out, scratch=(), aliases=None, cost=0, limit=24):
    return pl.pallas_call(
        kernel,
        out_shape=shape,
        in_specs=ins,
        out_specs=out,
        scratch_shapes=list(scratch),
        input_output_aliases=aliases or {},
        cost_estimate=pl.CostEstimate(flops=cost, bytes_accessed=cost // 100, transcendentals=0),
        compiler_params=pltpu.CompilerParams(vmem_limit_bytes=limit << 20),
    )


def bf16(*shape):
    return jax.ShapeDtypeStruct(shape, BF16)


def neighbour_swaps(count, cols):
    ids = lambda row, col: row * cols + col
    first = [(ids(r, c), ids(r ^ 1, c)) for r in range(count) for c in range(cols)]
    second = []
    for r in range(count):
        for c in range(cols):
            other = r + 1 if r % 2 else r - 1
            inside = 0 <= other < count
            second.append((ids(r, c), ids(other, c) if inside else ids(r, c ^ 1)))
    return first, second


def level(features, down_weight, bott_weight, up_weight, dec_weight):
    depth, chans, height, width = features.shape
    count, cols = lax.axis_size("row"), lax.axis_size("col")
    top = down_weight.shape[4]
    coarse, rows, each = width // 8, chans * height, bott_weight.shape[3]
    feat = features.reshape(depth, rows, width)

    sems = lambda n: pltpu.SemaphoreType.DMA((n,))
    scratch = [pltpu.VMEM(feat.shape, BF16), pltpu.VMEM(down_weight.shape, BF16)]
    up_one = [(i, i + 1) for i in range(cols - 1)]
    down_one = [(i + 1, i) for i in range(cols - 1)]
    paired = cols == 2 and top // 4 == width
    if paired:
        size = top // 4
        taps = bott_weight.shape[0] * bott_weight.shape[1] * bott_weight.shape[2] * each
        lowered, keep, give = call(
            functools.partial(lower_pair_kernel, count, chans, height),
            (bf16(2 * count, coarse // 2, 4 * each), bf16(taps, size), bf16(taps + rows, size)),
            [HBM] * 3,
            (VMEM,) * 3,
            scratch + [sems(depth + 4)],
            cost=1_000_000_000,
        )(fixed(feat), fixed(down_weight), fixed(bott_weight.reshape(taps, top)))
        took = lax.ppermute(give, "row", [(i, i ^ 1) for i in range(count)])
        got = lax.all_to_all(lowered, ("row", "col"), split_axis=0, concat_axis=0, tiled=True)
        shares = call(
            bottleneck_pair_kernel,
            bf16(2 * count, coarse, size),
            [VMEM] * 3,
            VMEM,
            [pltpu.VMEM(((count + 2) * coarse, 12 * each), BF16)],
            cost=2_000_000_000,
        )(got.reshape(count, 2, coarse // 2, 4 * each), keep, took)
        parts = lax.all_to_all(shares, ("row", "col"), split_axis=0, concat_axis=0, tiled=True)
    else:
        lowered = call(
            functools.partial(lower_kernel, count, chans, height),
            bf16(count, coarse, 3 * each),
            [HBM] * 2,
            VMEM,
            scratch + [sems(depth + 1)],
            cost=1_000_000_000,
        )(fixed(feat), fixed(down_weight))
        own = lax.all_to_all(lowered, "row", split_axis=0, concat_axis=0, tiled=True)
        shares = call(
            bottleneck_kernel,
            bf16(count, coarse, top),
            [VMEM] * 4,
            VMEM,
            [pltpu.VMEM(((count + 2) * coarse, 3 * each), BF16)] * 3,
            cost=2_000_000_000,
        )(lax.ppermute(own, "col", up_one), own, lax.ppermute(own, "col", down_one), bott_weight)
        parts = lax.all_to_all(shares, "row", split_axis=0, concat_axis=0, tiled=True)

    sides = 1 if cols == 2 else 2
    wide, *ends = call(
        functools.partial(outer_kernel, chans, height),
        (bf16(4 * width, top), bf16(rows // 2 if paired else rows, width), bf16(rows, width)),
        [VMEM] * 3,
        (VMEM,) * 3,
        [pltpu.VMEM((2, rows, width), F32)],
        cost=1_000_000_000,
    )(parts, feat, up_weight)
    joined, *sides = call(
        functools.partial(raise_kernel, chans, height),
        (bf16(depth, rows, width),) + (bf16(depth + (0 if paired else 2), chans, width),) * sides,
        [VMEM] * 3,
        (VMEM,) * (1 + sides),
        [pltpu.VMEM(feat.shape, F32)],
        cost=1_000_000_000,
    )(wide, feat, up_weight)
    if cols == 2:
        sides = [lax.ppermute(sides[0], "col", up_one + down_one)]
    else:
        sides = [lax.ppermute(sides[1], "col", up_one), lax.ppermute(sides[0], "col", down_one)]

    span = rows + 2 * chans
    band = call(
        functools.partial(band_kernel, chans, height),
        bf16(3 * rows, -(-3 * span // 128) * 128),
        [VMEM, HBM],
        VMEM,
        cost=500_000_000,
    )(dec_weight, joined)

    swapped = []
    for k, pairs in enumerate(neighbour_swaps(count, cols)):
        sent = ends[k] if paired else jnp.concatenate([ends[k]] + [side[depth + k] for side in sides], axis=0)
        swapped.append(lax.ppermute(sent, ("row", "col"), pairs))
    if paired:
        plane, corners = call(
            functools.partial(nearby_kernel, chans, height),
            (bf16(rows, width), bf16(2 * chans, width)),
            [VMEM] * 3,
            (VMEM,) * 2,
            [pltpu.VMEM((rows, width), F32)],
        )(took, *swapped)
        corners = lax.ppermute(corners, "col", up_one + down_one)
    else:
        got = [part for plane in swapped for part in (plane[:rows], plane[rows:])]

    shape = bf16(depth, rows, width)
    inner = call(
        functools.partial(interior_kernel, chans, height),
        bf16(depth - 2, rows, width),
        [VMEM] * (2 + len(sides)),
        VMEM,
        [
            pltpu.VMEM((height + 2, depth * chans, width), BF16),
            pltpu.VMEM((depth // 2 - 1, 2, rows, width), F32),
        ],
        cost=3_000_000_000,
    )(band, joined, *sides)
    field = pltpu.VMEM((height + 2, 6 * chans, width), BF16)
    spread, held = pltpu.VMEM((2, rows, width), F32), pltpu.VMEM((2, rows, width), BF16)
    if paired:
        values, partial = call(
            functools.partial(early_edge_kernel, chans, height),
            (jax.ShapeDtypeStruct((2, rows, width), F32), jax.ShapeDtypeStruct((3 * chans, 2 * width), F32)),
            [VMEM] * 5,
            (VMEM,) * 2,
            [field],
            cost=1_000_000_000,
        )(band, joined, plane, swapped[1], sides[0])
        decoded = call(
            functools.partial(late_edge_kernel, chans, height),
            shape,
            [VMEM] * 5,
            HBM,
            [pltpu.VMEM((256, 2 * width), BF16), spread, held, sems(3)],
            cost=1_000_000_000,
        )(band, corners, values, partial, inner)
    else:
        decoded = call(
            functools.partial(edge_kernel, chans, height),
            shape,
            [VMEM] * (7 + len(sides)),
            HBM,
            [field, spread, held, sems(3)],
            cost=1_000_000_000,
        )(band, joined, *got, *sides, inner)
    return decoded.reshape(depth, chans, height, width)


def solution(mesh):
    placed = (P("row", None, "col", None), P(), P(None, None, None, "row", None), P(), P())
    return jax.shard_map(level, mesh=mesh, in_specs=placed, out_specs=P("row", None, "col", None), check_vma=False)
```

```python
import functools

import jax
import jax.numpy as jnp
from jax import lax
from jax.experimental import pallas as pl
from jax.experimental.pallas import tpu as pltpu
from jax.sharding import PartitionSpec as P


F32, BF16 = jnp.float32, jnp.bfloat16
NT = (((1,), (1,)), ((), ()))


def iota(shape, dim):
    return lax.broadcasted_iota(jnp.int32, shape, dim)


def dot(a, b):
    return jnp.dot(a, b, preferred_element_type=F32)


def dot_nt(a, b):
    return lax.dot_general(a, b, NT, preferred_element_type=F32)


def tiled(piece, shape):
    rows, lanes = (size // part for size, part in zip(shape, piece.shape))
    return jnp.concatenate([jnp.concatenate([piece] * lanes, axis=1)] * rows, axis=0)


def silu(v):
    half = 0.5 * v
    return half + half * jnp.tanh(half)


def lowered_rows(height, chans, loads, feat, down):
    planes, rows, width = feat.shape
    quarters = planes // 2
    coarse = width // 8
    top = down.shape[4]
    shape = (height // 2 * chans, rows)
    r, c = iota(shape, 0), iota(shape, 1)
    pick = ((r % chans == c // height) & (r // chans == (c % height) // 2)).astype(F32).astype(BF16)
    shape = (4 * coarse, width)
    r, c = iota(shape, 0), iota(shape, 1)
    cols = ((r % coarse == c // 8) & (r // coarse == (c % 8) // 2)).astype(F32).astype(BF16)
    loads[0].wait()
    tables = [(dot(pick, feat[2 * a]) + dot(pick, feat[2 * a + 1])).astype(BF16) for a in range(quarters)]
    pooled = [(dot_nt(cols, table) * 0.125).astype(BF16) for table in tables]
    low = jnp.zeros((coarse, top), F32)
    for a in range(quarters):
        for load in loads[1 + 2 * a : 3 + 2 * a]:
            load.wait()
        for c in range(4):
            low = low + dot(pooled[a][c * coarse : (c + 1) * coarse], down[a, :, c].reshape(-1, top))
    return silu(low)


def input_loads(feat_hbm, down_hbm, feat, down, sems):
    taps, half = down.shape[0], down.shape[1] // 2
    loads = [pltpu.make_async_copy(feat_hbm, feat, sems.at[0])]
    for a in range(taps):
        for part in (slice(0, half), slice(half, 2 * half)):
            loads.append(pltpu.make_async_copy(down_hbm.at[a, part], down.at[a, part], sems.at[len(loads)]))
    return loads


def lower_kernel(count, chans, height, feat_hbm, down_hbm, out, feat, down, sems):
    loads = input_loads(feat_hbm, down_hbm, feat, down, sems)
    for load in loads:
        load.start()
    low = lowered_rows(height, chans, loads, feat, down)
    coarse = low.shape[0]
    each = low.shape[1] // count
    place = iota(low.shape, 0)
    before = jnp.where(place == 0, 0.0, pltpu.roll(low, 1, 0))
    after = jnp.where(place == coarse - 1, 0.0, pltpu.roll(low, coarse - 1, 0))
    for k in range(count):
        part = slice(k * each, (k + 1) * each)
        out[k] = jnp.concatenate([before[:, part], low[:, part], after[:, part]], axis=1).astype(BF16)


def quarter(row, col, size):
    return pl.multiple_of((2 * (row % 2) + col) * size, size)


def lower_pair_kernel(count, chans, height, feat_hbm, down_hbm, bott_hbm, out, keep, give, feat, down, sems):
    loads = input_loads(feat_hbm, down_hbm, feat, down, sems)
    row, col = lax.axis_index("row"), lax.axis_index("col")
    taps, size = keep.shape
    edge = (feat.shape[0] - 1) * (1 - row % 2)
    quarters = [
        pltpu.make_async_copy(
            bott_hbm.at[:, pl.ds(quarter(row + 1, col, size), size)], give.at[:taps], sems.at[len(loads)]
        ),
        pltpu.make_async_copy(feat_hbm.at[edge], give.at[taps:], sems.at[len(loads) + 1]),
        pltpu.make_async_copy(
            bott_hbm.at[:, pl.ds(quarter(row, col, size), size)], keep, sems.at[len(loads) + 2]
        ),
    ]
    for load in loads + quarters:
        load.start()
    low = lowered_rows(height, chans, loads, feat, down)
    half = low.shape[0] // 2
    each = low.shape[1] // count
    for k in range(count):
        pieces = []
        for rows in (slice(0, half), slice(half, 2 * half)):
            for owner in (k, k ^ 1):
                pieces.append(low[rows, owner * each : (owner + 1) * each])
        block = jnp.concatenate(pieces, axis=1).astype(BF16)
        out[2 * k] = block
        out[2 * k + 1] = block
    for load in quarters:
        load.wait()


def bottleneck_kernel(*refs):
    blocks, weight, out, pads = refs[:3], refs[3], refs[4], refs[5:]
    depth, coarse, top = out.shape
    rows = depth * coarse
    lanes = 3 * weight.shape[3]
    total = jnp.zeros((rows, top), F32)
    for tap, (block, pad) in enumerate(zip(blocks, pads)):
        zero = jnp.zeros((coarse, lanes), BF16)
        pad[:coarse] = zero
        pad[coarse + rows :] = zero
        pad[coarse : coarse + rows] = block[...].reshape(rows, lanes)
        for a in range(3):
            kernel = weight[a, tap].reshape(lanes, top)
            total = total + dot(pad[a * coarse : a * coarse + rows], kernel)
    out[...] = total.astype(BF16).reshape(out.shape)


def bottleneck_pair_kernel(got, keep, took, out, pad):
    depth, _, half, lanes = got.shape
    group = lanes // 2
    coarse = 2 * half
    rows = depth * coarse
    each = group // 2
    lane = iota((half, lanes), 1)
    blocks = []
    for d in range(depth):
        low, high = got[d, 0].astype(F32), got[d, 1].astype(F32)
        blocks.append(jnp.where(lane < group, low, pltpu.roll(high, group, 1)))
        blocks.append(jnp.where(lane < group, pltpu.roll(low, group, 1), high))
    here = jnp.concatenate(blocks, axis=0)
    place = tiled(iota((coarse, lanes), 0), (rows, lanes))
    before = jnp.where(place == 0, 0.0, pltpu.roll(here, 1, 0))
    after = jnp.where(place == coarse - 1, 0.0, pltpu.roll(here, rows - 1, 0))
    zero = jnp.zeros((coarse, 3 * lanes), BF16)
    pad[:coarse] = zero
    pad[coarse + rows :] = zero
    for c, value in enumerate((before, here, after)):
        pad[coarse : coarse + rows, c * lanes : (c + 1) * lanes] = value.astype(BF16)
    total = None
    for a in range(3):
        bands = []
        for c in range(3):
            for source in range(2):
                for held in (keep, took):
                    at = [((3 * a + source - h + 1) * 3 + c) * each for h in range(2)]
                    bands.append(jnp.concatenate([held[k : k + each] for k in at], axis=1))
        term = dot(pad[a * coarse : a * coarse + rows], jnp.concatenate(bands, axis=0))
        total = term if total is None else total + term
    size = out.shape[2]
    for h in range(2):
        for d in range(depth):
            out[2 * d + h] = total[d * coarse : (d + 1) * coarse, h * size : (h + 1) * size].astype(BF16)


def join(chans, height, plane, raised, spread, store):
    spread[...] = plane.astype(F32)
    for h in range(height):
        at = (h // 2) * chans
        value = spread[pl.ds(h, chans, stride=height), :] + raised[at : at + chans].astype(F32)
        store(h * chans, value.astype(BF16))


def outer_kernel(chans, height, parts, feat, up, wide, first, second, spread):
    planes, rows, width = feat.shape
    coarse, top = width // 8, up.shape[4]
    groups = top // parts.shape[2]
    sums = []
    for q in range(groups):
        total = parts[q].astype(F32)
        for k in range(q + groups, parts.shape[0], groups):
            total = total + parts[k].astype(F32)
        sums.append(total)
    middle = silu(sums[0] if groups == 1 else jnp.concatenate(sums, axis=1))
    spreading = jnp.concatenate([jnp.broadcast_to(middle[w : w + 1], (8, top)) for w in range(coarse)], axis=0)
    spreading = spreading.astype(BF16)
    which = iota((16, 128), 0) % 8 // 2
    masks = [tiled((which == c).astype(F32).astype(BF16), spreading.shape) for c in range(4)]
    odd = lax.axis_index("row") % 2
    last = up.shape[0] - 1
    steps = (last * (1 - odd), last * odd)
    raised = None
    for c in range(4):
        columns = spreading * masks[c]
        wide[c * width : (c + 1) * width] = columns
        weight = jnp.concatenate([up[a, :, c].reshape(-1, top) for a in steps], axis=0)
        term = dot_nt(weight, columns)
        raised = term if raised is None else raised + term
    per = raised.shape[0] // 2

    def put(target):
        def store(at, value):
            target[at : at + chans] = value

        return store

    if first.shape[0] == rows:
        join(chans, height, feat[(planes - 1) * (1 - odd)], raised[:per], spread.at[0], put(first))
    else:
        first[...] = raised[:per].astype(BF16)
    join(chans, height, feat[(planes - 1) * odd], raised[per:], spread.at[1], put(second))


def raise_kernel(chans, height, wide, feat, up, joined, *rest):
    sides, spread = rest[:-1], rest[-1]
    planes, rows, width = feat.shape
    raised = None
    for c in range(4):
        weight = up[:, :, c].reshape(-1, up.shape[4])
        term = dot_nt(weight, wide[c * width : (c + 1) * width])
        raised = term if raised is None else raised + term
    per = chans * (height // 2)
    for d in range(planes):

        def store(at, value):
            joined[d, at : at + chans] = value

        join(chans, height, feat[d], raised[d // 2 * per : (d // 2 + 1) * per], spread.at[d], store)
    odd = lax.axis_index("row") % 2
    near, far = (planes - 1) * (1 - odd), (planes - 1) * odd
    if len(sides) == 1:
        starts = [pl.multiple_of((rows - chans) * (1 - lax.axis_index("col")), chans)]
    else:
        starts = [0, rows - chans]
    for side, start in zip(sides, starts):
        for d in range(planes):
            side[d] = joined[d, pl.ds(start, chans)]
        if side.shape[0] > planes:
            side[planes] = joined[near, pl.ds(start, chans)]
            side[planes + 1] = joined[far, pl.ds(start, chans)]


def band_kernel(chans, height, dec, after, out):
    eye = (iota((chans, chans), 0) == iota((chans, chans), 1)).astype(F32).astype(BF16)
    step = 3 * chans
    wide = out.shape[1]
    for c in range(3):
        taps = [dot_nt(eye, dec[:, b, c].reshape(step, chans)) for b in range(3)]
        base = jnp.concatenate(taps + [jnp.zeros((chans, wide - 3 * step), F32)], axis=1)
        for h in range(height):
            row = h * step + c * chans
            moved = base if h == 0 else pltpu.roll(base, h * step, 1)
            out[row : row + chans] = moved.astype(BF16)


def taps_of(chans, part):
    width = part.shape[1]
    lane = iota((chans, width), 1)
    before = jnp.where(lane == 0, 0.0, pltpu.roll(part[:chans], 1, 1))
    after = jnp.where(lane == width - 1, 0.0, pltpu.roll(part[2 * chans :], width - 1, 1))
    return silu(part[chans : 2 * chans] + before + after)


def decode_pair(chans, height, band, planes, spread, store):
    step = 3 * chans
    blocks = [jnp.concatenate([plane(h) for plane in planes], axis=1) for h in range(height + 2)]
    window = jnp.concatenate(blocks, axis=0)
    width = window.shape[1] // 2
    sums = [None] * height
    for at in range(0, window.shape[0], 256):
        stop = min(at + 256, window.shape[0])
        first = max(0, at // step - 2)
        last = min(height - 1, (stop - 1) // step)
        part = dot(band[first * step : (last + 1) * step, at:stop], window[at:stop])
        for h in range(first, last + 1):
            piece = part[(h - first) * step : (h - first + 1) * step]
            sums[h] = piece if sums[h] is None else sums[h] + piece
    for e in range(2):
        for h in range(height):
            value = taps_of(chans, sums[h][:, e * width : (e + 1) * width])
            spread[e, pl.ds(h, chans, stride=height), :] = value
        store(e)
    return sums


def fill(field, slot, chans, plane, borders):
    height = field.shape[0]
    at = slice(slot * chans, (slot + 1) * chans)
    for h in range(1, height - 1):
        field[h, at] = plane[(h - 1) * chans : h * chans]
    if len(borders) == 1:
        col = lax.axis_index("col")
        field[(height - 1) * col, at] = jnp.zeros_like(borders[0])
        field[(height - 1) * (1 - col), at] = borders[0]
    else:
        field[0, at] = borders[0]
        field[height - 1, at] = borders[1]


def interior_kernel(chans, height, band, joined, *rest):
    sides, (out, field, spread) = rest[:-3], rest[-3:]
    planes = joined.shape[0]
    for d in range(planes):
        fill(field, d, chans, joined[d], [side[d] for side in sides])
    for step in range(planes // 2 - 1):
        views = [lambda h, at=(2 * step + e) * chans: field[h, at : at + 3 * chans] for e in range(2)]

        def store(e):
            out[2 * step + e] = spread[step, e].astype(BF16)

        decode_pair(chans, height, band, views, spread.at[step], store)


def nearby_kernel(chans, height, took, near, far, plane, corners, spread):
    rows = plane.shape[0]

    def store(at, value):
        plane[at : at + chans] = value

    join(chans, height, took[-rows:], near, spread, store)
    start = pl.multiple_of((rows - chans) * (1 - lax.axis_index("col")), chans)
    corners[:chans] = plane[pl.ds(start, chans)]
    corners[chans:] = far[pl.ds(start, chans)]


def fill_edges(chans, joined, near, far, sides, near_rows, far_rows, field):
    planes, _, width = joined.shape
    for slot, d in ((1, 0), (2, 1), (3, planes - 2), (4, planes - 1)):
        fill(field, slot, chans, joined[d], [side[d] for side in sides])
    row, last = lax.axis_index("row"), lax.axis_size("row") - 1

    def outer(slot, plane, corners):
        fill(field, slot, chans, plane[...], corners)

    @pl.when(row % 2 == 0)
    def _():
        outer(0, far, far_rows)
        outer(5, near, near_rows)

    @pl.when(row % 2 == 1)
    def _():
        outer(0, near, near_rows)
        outer(5, far, far_rows)

    @pl.when(row == 0)
    def _():
        field[:, :chans] = jnp.zeros((field.shape[0], chans, width), BF16)

    @pl.when(row == last)
    def _():
        field[:, 5 * chans :] = jnp.zeros((field.shape[0], chans, width), BF16)


def edge_views(chans, field):
    return [lambda h, at=3 * e * chans: field[h, at : at + 3 * chans] for e in range(2)]


def result_copies(inner, held, out_hbm, sems):
    last = out_hbm.shape[0] - 1
    pieces = ((inner, out_hbm.at[1:last]), (held.at[0], out_hbm.at[0]), (held.at[1], out_hbm.at[last]))
    return [pltpu.make_async_copy(piece, place, sems.at[k]) for k, (piece, place) in enumerate(pieces)]


def edge_kernel(chans, height, band, joined, near, near_rows, far, far_rows, *rest):
    sides, (inner, out_hbm, field, spread, held, sems) = rest[:-6], rest[-6:]
    copies = result_copies(inner, held, out_hbm, sems)
    copies[0].start()
    borders = [[got[k * chans : (k + 1) * chans] for k in range(len(sides))] for got in (near_rows, far_rows)]
    fill_edges(chans, joined, near, far, sides, *borders, field)

    def store(e):
        held[e] = spread[e].astype(BF16)
        copies[1 + e].start()

    decode_pair(chans, height, band, edge_views(chans, field), spread, store)
    for copy in copies:
        copy.wait()


def early_edge_kernel(chans, height, band, joined, near, far, side, values, partial, field):
    none = [jnp.zeros((chans, joined.shape[2]), BF16)]
    fill_edges(chans, joined, near, far, [side], none, none, field)
    sums = decode_pair(chans, height, band, edge_views(chans, field), values, lambda e: None)
    partial[...] = jnp.where(lax.axis_index("col") == 0, sums[-1], sums[0])


def late_edge_kernel(chans, height, band, corners, values, partial, inner, out_hbm, window, spread, held, sems):
    copies = result_copies(inner, held, out_hbm, sems)
    copies[0].start()
    row, last, col = lax.axis_index("row"), lax.axis_size("row") - 1, lax.axis_index("col")
    step, width = 3 * chans, corners.shape[1]
    tile = window.shape[0]
    at_tile = pl.multiple_of((height + 2) * step // tile * tile * (1 - col), tile)
    at_row = (height + 1) * step % tile * (1 - col)
    window[...] = jnp.zeros(window.shape, BF16)

    def put(tap, got):
        window[pl.ds(pl.multiple_of(at_row + tap * chans, chans), chans), tap // 2 * width : (tap // 2 + 1) * width] = got

    even = row % 2 == 0

    @pl.when((row > 0) & even)
    def _():
        put(0, corners[chans:])

    @pl.when((row > 0) & ~even)
    def _():
        put(0, corners[:chans])

    @pl.when((row < last) & even)
    def _():
        put(2, corners[:chans])

    @pl.when((row < last) & ~even)
    def _():
        put(2, corners[chans:])

    edge = (height - 1) * (1 - col)
    kernel = band[pl.ds(pl.multiple_of(edge * step, step), step), pl.ds(at_tile, tile)]
    sums = partial[...] + dot(kernel, window[...])
    for e in range(2):
        spread[e] = values[e]
        spread[e, pl.ds(edge, chans, stride=height), :] = taps_of(chans, sums[:, e * width : (e + 1) * width])
        held[e] = spread[e].astype(BF16)
        copies[1 + e].start()
    for copy in copies:
        copy.wait()


VMEM = pl.BlockSpec(memory_space=pltpu.MemorySpace.VMEM)
HBM = pl.BlockSpec(memory_space=pltpu.MemorySpace.HBM)


def fixed(x):
    return pltpu.with_memory_space_constraint(x, pltpu.MemorySpace.HBM)


def call(kernel, shape, ins, out, scratch=(), aliases=None, cost=0, limit=24):
    return pl.pallas_call(
        kernel,
        out_shape=shape,
        in_specs=ins,
        out_specs=out,
        scratch_shapes=list(scratch),
        input_output_aliases=aliases or {},
        cost_estimate=pl.CostEstimate(flops=cost, bytes_accessed=cost // 100, transcendentals=0),
        compiler_params=pltpu.CompilerParams(vmem_limit_bytes=limit << 20),
    )


def bf16(*shape):
    return jax.ShapeDtypeStruct(shape, BF16)


def neighbour_swaps(count, cols):
    ids = lambda row, col: row * cols + col
    first = [(ids(r, c), ids(r ^ 1, c)) for r in range(count) for c in range(cols)]
    second = []
    for r in range(count):
        for c in range(cols):
            other = r + 1 if r % 2 else r - 1
            inside = 0 <= other < count
            second.append((ids(r, c), ids(other, c) if inside else ids(r, c ^ 1)))
    return first, second


def level(features, down_weight, bott_weight, up_weight, dec_weight):
    depth, chans, height, width = features.shape
    count, cols = lax.axis_size("row"), lax.axis_size("col")
    top = down_weight.shape[4]
    coarse, rows, each = width // 8, chans * height, bott_weight.shape[3]
    feat = features.reshape(depth, rows, width)

    sems = lambda n: pltpu.SemaphoreType.DMA((n,))
    scratch = [pltpu.VMEM(feat.shape, BF16), pltpu.VMEM(down_weight.shape, BF16)]
    up_one = [(i, i + 1) for i in range(cols - 1)]
    down_one = [(i + 1, i) for i in range(cols - 1)]
    paired = cols == 2 and top // 4 == width
    if paired:
        size = top // 4
        taps = bott_weight.shape[0] * bott_weight.shape[1] * bott_weight.shape[2] * each
        lowered, keep, give = call(
            functools.partial(lower_pair_kernel, count, chans, height),
            (bf16(2 * count, coarse // 2, 4 * each), bf16(taps, size), bf16(taps + rows, size)),
            [HBM] * 3,
            (VMEM,) * 3,
            scratch + [sems(depth + 4)],
            cost=1_000_000_000,
        )(fixed(feat), fixed(down_weight), fixed(bott_weight.reshape(taps, top)))
        took = lax.ppermute(give, "row", [(i, i ^ 1) for i in range(count)])
        got = lax.all_to_all(lowered, ("row", "col"), split_axis=0, concat_axis=0, tiled=True)
        shares = call(
            bottleneck_pair_kernel,
            bf16(2 * count, coarse, size),
            [VMEM] * 3,
            VMEM,
            [pltpu.VMEM(((count + 2) * coarse, 12 * each), BF16)],
            cost=2_000_000_000,
        )(got.reshape(count, 2, coarse // 2, 4 * each), keep, took)
        parts = lax.all_to_all(shares, ("row", "col"), split_axis=0, concat_axis=0, tiled=True)
    else:
        lowered = call(
            functools.partial(lower_kernel, count, chans, height),
            bf16(count, coarse, 3 * each),
            [HBM] * 2,
            VMEM,
            scratch + [sems(depth + 1)],
            cost=1_000_000_000,
        )(fixed(feat), fixed(down_weight))
        own = lax.all_to_all(lowered, "row", split_axis=0, concat_axis=0, tiled=True)
        shares = call(
            bottleneck_kernel,
            bf16(count, coarse, top),
            [VMEM] * 4,
            VMEM,
            [pltpu.VMEM(((count + 2) * coarse, 3 * each), BF16)] * 3,
            cost=2_000_000_000,
        )(lax.ppermute(own, "col", up_one), own, lax.ppermute(own, "col", down_one), bott_weight)
        parts = lax.all_to_all(shares, "row", split_axis=0, concat_axis=0, tiled=True)

    sides = 1 if cols == 2 else 2
    wide, *ends = call(
        functools.partial(outer_kernel, chans, height),
        (bf16(4 * width, top), bf16(rows // 2 if paired else rows, width), bf16(rows, width)),
        [VMEM] * 3,
        (VMEM,) * 3,
        [pltpu.VMEM((2, rows, width), F32)],
        cost=1_000_000_000,
    )(parts, feat, up_weight)
    joined, *sides = call(
        functools.partial(raise_kernel, chans, height),
        (bf16(depth, rows, width),) + (bf16(depth + (0 if paired else 2), chans, width),) * sides,
        [VMEM] * 3,
        (VMEM,) * (1 + sides),
        [pltpu.VMEM(feat.shape, F32)],
        cost=1_000_000_000,
    )(wide, feat, up_weight)
    if cols == 2:
        sides = [lax.ppermute(sides[0], "col", up_one + down_one)]
    else:
        sides = [lax.ppermute(sides[1], "col", up_one), lax.ppermute(sides[0], "col", down_one)]

    span = rows + 2 * chans
    band = call(
        functools.partial(band_kernel, chans, height),
        bf16(3 * rows, -(-3 * span // 128) * 128),
        [VMEM, HBM],
        VMEM,
        cost=500_000_000,
    )(dec_weight, joined)

    swapped = []
    for k, pairs in enumerate(neighbour_swaps(count, cols)):
        sent = ends[k] if paired else jnp.concatenate([ends[k]] + [side[depth + k] for side in sides], axis=0)
        swapped.append(lax.ppermute(sent, ("row", "col"), pairs))
    if paired:
        plane, corners = call(
            functools.partial(nearby_kernel, chans, height),
            (bf16(rows, width), bf16(2 * chans, width)),
            [VMEM] * 3,
            (VMEM,) * 2,
            [pltpu.VMEM((rows, width), F32)],
        )(took, *swapped)
        corners = lax.ppermute(corners, "col", up_one + down_one)
    else:
        got = [part for plane in swapped for part in (plane[:rows], plane[rows:])]

    shape = bf16(depth, rows, width)
    inner = call(
        functools.partial(interior_kernel, chans, height),
        bf16(depth - 2, rows, width),
        [VMEM] * (2 + len(sides)),
        VMEM,
        [
            pltpu.VMEM((height + 2, depth * chans, width), BF16),
            pltpu.VMEM((depth // 2 - 1, 2, rows, width), F32),
        ],
        cost=3_000_000_000,
    )(band, joined, *sides)
    field = pltpu.VMEM((height + 2, 6 * chans, width), BF16)
    spread, held = pltpu.VMEM((2, rows, width), F32), pltpu.VMEM((2, rows, width), BF16)
    if paired:
        values, partial = call(
            functools.partial(early_edge_kernel, chans, height),
            (jax.ShapeDtypeStruct((2, rows, width), F32), jax.ShapeDtypeStruct((3 * chans, 2 * width), F32)),
            [VMEM] * 5,
            (VMEM,) * 2,
            [field],
            cost=1_000_000_000,
        )(band, joined, plane, swapped[1], sides[0])
        decoded = call(
            functools.partial(late_edge_kernel, chans, height),
            shape,
            [VMEM] * 5,
            HBM,
            [pltpu.VMEM((256, 2 * width), BF16), spread, held, sems(3)],
            cost=1_000_000_000,
        )(band, corners, values, partial, inner)
    else:
        decoded = call(
            functools.partial(edge_kernel, chans, height),
            shape,
            [VMEM] * (7 + len(sides)),
            HBM,
            [field, spread, held, sems(3)],
            cost=1_000_000_000,
        )(band, joined, *got, *sides, inner)
    return decoded.reshape(depth, chans, height, width)


def solution(mesh):
    placed = (P("row", None, "col", None), P(), P(None, None, None, "row", None), P(), P())
    return jax.shard_map(level, mesh=mesh, in_specs=placed, out_specs=P("row", None, "col", None), check_vma=False)
```

```python
import functools

import jax
import jax.numpy as jnp
from jax import lax
from jax.experimental import pallas as pl
from jax.experimental.pallas import tpu as pltpu
from jax.sharding import PartitionSpec as P


F32, BF16 = jnp.float32, jnp.bfloat16
NT = (((1,), (1,)), ((), ()))


def iota(shape, dim):
    return lax.broadcasted_iota(jnp.int32, shape, dim)


def dot(a, b):
    return jnp.dot(a, b, preferred_element_type=F32)


def dot_nt(a, b):
    return lax.dot_general(a, b, NT, preferred_element_type=F32)


def tiled(piece, shape):
    rows, lanes = (size // part for size, part in zip(shape, piece.shape))
    return jnp.concatenate([jnp.concatenate([piece] * lanes, axis=1)] * rows, axis=0)


def silu(v):
    half = 0.5 * v
    return half + half * jnp.tanh(half)


def lowered_rows(height, chans, loads, feat, down):
    planes, rows, width = feat.shape
    quarters = planes // 2
    coarse = width // 8
    top = down.shape[4]
    shape = (height // 2 * chans, rows)
    r, c = iota(shape, 0), iota(shape, 1)
    pick = ((r % chans == c // height) & (r // chans == (c % height) // 2)).astype(F32).astype(BF16)
    shape = (4 * coarse, width)
    r, c = iota(shape, 0), iota(shape, 1)
    cols = ((r % coarse == c // 8) & (r // coarse == (c % 8) // 2)).astype(F32).astype(BF16)
    loads[0].wait()
    tables = [(dot(pick, feat[2 * a]) + dot(pick, feat[2 * a + 1])).astype(BF16) for a in range(quarters)]
    pooled = [(dot_nt(cols, table) * 0.125).astype(BF16) for table in tables]
    low = jnp.zeros((coarse, top), F32)
    for a in range(quarters):
        for load in loads[1 + 2 * a : 3 + 2 * a]:
            load.wait()
        for c in range(4):
            low = low + dot(pooled[a][c * coarse : (c + 1) * coarse], down[a, :, c].reshape(-1, top))
    return silu(low)


def input_loads(feat_hbm, down_hbm, feat, down, sems):
    taps, half = down.shape[0], down.shape[1] // 2
    loads = [pltpu.make_async_copy(feat_hbm, feat, sems.at[0])]
    for a in range(taps):
        for part in (slice(0, half), slice(half, 2 * half)):
            loads.append(pltpu.make_async_copy(down_hbm.at[a, part], down.at[a, part], sems.at[len(loads)]))
    return loads


def lower_kernel(count, chans, height, feat_hbm, down_hbm, out, feat, down, sems):
    loads = input_loads(feat_hbm, down_hbm, feat, down, sems)
    for load in loads:
        load.start()
    low = lowered_rows(height, chans, loads, feat, down)
    coarse = low.shape[0]
    each = low.shape[1] // count
    place = iota(low.shape, 0)
    before = jnp.where(place == 0, 0.0, pltpu.roll(low, 1, 0))
    after = jnp.where(place == coarse - 1, 0.0, pltpu.roll(low, coarse - 1, 0))
    for k in range(count):
        part = slice(k * each, (k + 1) * each)
        out[k] = jnp.concatenate([before[:, part], low[:, part], after[:, part]], axis=1).astype(BF16)


def quarter(row, col, size):
    return pl.multiple_of((2 * (row % 2) + col) * size, size)


def lower_pair_kernel(count, chans, height, feat_hbm, down_hbm, bott_hbm, out, keep, give, feat, down, sems):
    loads = input_loads(feat_hbm, down_hbm, feat, down, sems)
    row, col = lax.axis_index("row"), lax.axis_index("col")
    taps, size = keep.shape
    edge = (feat.shape[0] - 1) * (1 - row % 2)
    quarters = [
        pltpu.make_async_copy(
            bott_hbm.at[:, pl.ds(quarter(row + 1, col, size), size)], give.at[:taps], sems.at[len(loads)]
        ),
        pltpu.make_async_copy(feat_hbm.at[edge], give.at[taps:], sems.at[len(loads) + 1]),
        pltpu.make_async_copy(
            bott_hbm.at[:, pl.ds(quarter(row, col, size), size)], keep, sems.at[len(loads) + 2]
        ),
    ]
    for load in loads + quarters:
        load.start()
    low = lowered_rows(height, chans, loads, feat, down)
    half = low.shape[0] // 2
    each = low.shape[1] // count
    for k in range(count):
        pieces = []
        for rows in (slice(0, half), slice(half, 2 * half)):
            for owner in (k, k ^ 1):
                pieces.append(low[rows, owner * each : (owner + 1) * each])
        block = jnp.concatenate(pieces, axis=1).astype(BF16)
        out[2 * k] = block
        out[2 * k + 1] = block
    for load in quarters:
        load.wait()


def bottleneck_kernel(*refs):
    blocks, weight, out, pads = refs[:3], refs[3], refs[4], refs[5:]
    depth, coarse, top = out.shape
    rows = depth * coarse
    lanes = 3 * weight.shape[3]
    total = jnp.zeros((rows, top), F32)
    for tap, (block, pad) in enumerate(zip(blocks, pads)):
        zero = jnp.zeros((coarse, lanes), BF16)
        pad[:coarse] = zero
        pad[coarse + rows :] = zero
        pad[coarse : coarse + rows] = block[...].reshape(rows, lanes)
        for a in range(3):
            kernel = weight[a, tap].reshape(lanes, top)
            total = total + dot(pad[a * coarse : a * coarse + rows], kernel)
    out[...] = total.astype(BF16).reshape(out.shape)


def bottleneck_pair_kernel(got, keep, took, out, pad):
    depth, _, half, lanes = got.shape
    group = lanes // 2
    coarse = 2 * half
    rows = depth * coarse
    each = group // 2
    lane = iota((half, lanes), 1)
    blocks = []
    for d in range(depth):
        low, high = got[d, 0].astype(F32), got[d, 1].astype(F32)
        blocks.append(jnp.where(lane < group, low, pltpu.roll(high, group, 1)))
        blocks.append(jnp.where(lane < group, pltpu.roll(low, group, 1), high))
    here = jnp.concatenate(blocks, axis=0)
    place = tiled(iota((coarse, lanes), 0), (rows, lanes))
    before = jnp.where(place == 0, 0.0, pltpu.roll(here, 1, 0))
    after = jnp.where(place == coarse - 1, 0.0, pltpu.roll(here, rows - 1, 0))
    zero = jnp.zeros((coarse, 3 * lanes), BF16)
    pad[:coarse] = zero
    pad[coarse + rows :] = zero
    for c, value in enumerate((before, here, after)):
        pad[coarse : coarse + rows, c * lanes : (c + 1) * lanes] = value.astype(BF16)
    total = None
    for a in range(3):
        bands = []
        for c in range(3):
            for source in range(2):
                for held in (keep, took):
                    at = [((3 * a + source - h + 1) * 3 + c) * each for h in range(2)]
                    bands.append(jnp.concatenate([held[k : k + each] for k in at], axis=1))
        term = dot(pad[a * coarse : a * coarse + rows], jnp.concatenate(bands, axis=0))
        total = term if total is None else total + term
    size = out.shape[2]
    for h in range(2):
        for d in range(depth):
            out[2 * d + h] = total[d * coarse : (d + 1) * coarse, h * size : (h + 1) * size].astype(BF16)


def join(chans, height, plane, raised, spread, store):
    spread[...] = plane.astype(F32)
    for h in range(height):
        at = (h // 2) * chans
        value = spread[pl.ds(h, chans, stride=height), :] + raised[at : at + chans].astype(F32)
        store(h * chans, value.astype(BF16))


def outer_kernel(chans, height, parts, feat, up, wide, first, second, spread):
    planes, rows, width = feat.shape
    coarse, top = width // 8, up.shape[4]
    groups = top // parts.shape[2]
    sums = []
    for q in range(groups):
        total = parts[q].astype(F32)
        for k in range(q + groups, parts.shape[0], groups):
            total = total + parts[k].astype(F32)
        sums.append(total)
    middle = silu(sums[0] if groups == 1 else jnp.concatenate(sums, axis=1))
    spreading = jnp.concatenate([jnp.broadcast_to(middle[w : w + 1], (8, top)) for w in range(coarse)], axis=0)
    spreading = spreading.astype(BF16)
    which = iota((16, 128), 0) % 8 // 2
    masks = [tiled((which == c).astype(F32).astype(BF16), spreading.shape) for c in range(4)]
    odd = lax.axis_index("row") % 2
    last = up.shape[0] - 1
    steps = (last * (1 - odd), last * odd)
    raised = None
    for c in range(4):
        columns = spreading * masks[c]
        wide[c * width : (c + 1) * width] = columns
        weight = jnp.concatenate([up[a, :, c].reshape(-1, top) for a in steps], axis=0)
        term = dot_nt(weight, columns)
        raised = term if raised is None else raised + term
    per = raised.shape[0] // 2

    def put(target):
        def store(at, value):
            target[at : at + chans] = value

        return store

    if first.shape[0] == rows:
        join(chans, height, feat[(planes - 1) * (1 - odd)], raised[:per], spread.at[0], put(first))
    else:
        first[...] = raised[:per].astype(BF16)
    join(chans, height, feat[(planes - 1) * odd], raised[per:], spread.at[1], put(second))


def raise_kernel(chans, height, wide, feat, up, joined, *rest):
    sides, spread = rest[:-1], rest[-1]
    planes, rows, width = feat.shape
    raised = None
    for c in range(4):
        weight = up[:, :, c].reshape(-1, up.shape[4])
        term = dot_nt(weight, wide[c * width : (c + 1) * width])
        raised = term if raised is None else raised + term
    per = chans * (height // 2)
    for d in range(planes):

        def store(at, value):
            joined[d, at : at + chans] = value

        join(chans, height, feat[d], raised[d // 2 * per : (d // 2 + 1) * per], spread.at[d], store)
    odd = lax.axis_index("row") % 2
    near, far = (planes - 1) * (1 - odd), (planes - 1) * odd
    if len(sides) == 1:
        starts = [pl.multiple_of((rows - chans) * (1 - lax.axis_index("col")), chans)]
    else:
        starts = [0, rows - chans]
    for side, start in zip(sides, starts):
        for d in range(planes):
            side[d] = joined[d, pl.ds(start, chans)]
        if side.shape[0] > planes:
            side[planes] = joined[near, pl.ds(start, chans)]
            side[planes + 1] = joined[far, pl.ds(start, chans)]


def band_kernel(chans, height, dec, after, out):
    eye = (iota((chans, chans), 0) == iota((chans, chans), 1)).astype(F32).astype(BF16)
    step = 3 * chans
    wide = out.shape[1]
    for c in range(3):
        taps = [dot_nt(eye, dec[:, b, c].reshape(step, chans)) for b in range(3)]
        base = jnp.concatenate(taps + [jnp.zeros((chans, wide - 3 * step), F32)], axis=1)
        for h in range(height):
            row = h * step + c * chans
            moved = base if h == 0 else pltpu.roll(base, h * step, 1)
            out[row : row + chans] = moved.astype(BF16)


def taps_of(chans, part):
    width = part.shape[1]
    lane = iota((chans, width), 1)
    before = jnp.where(lane == 0, 0.0, pltpu.roll(part[:chans], 1, 1))
    after = jnp.where(lane == width - 1, 0.0, pltpu.roll(part[2 * chans :], width - 1, 1))
    return silu(part[chans : 2 * chans] + before + after)


def decode_pair(chans, height, band, planes, spread, store):
    step = 3 * chans
    blocks = [jnp.concatenate([plane(h) for plane in planes], axis=1) for h in range(height + 2)]
    window = jnp.concatenate(blocks, axis=0)
    width = window.shape[1] // 2
    sums = [None] * height
    for at in range(0, window.shape[0], 256):
        stop = min(at + 256, window.shape[0])
        first = max(0, at // step - 2)
        last = min(height - 1, (stop - 1) // step)
        part = dot(band[first * step : (last + 1) * step, at:stop], window[at:stop])
        for h in range(first, last + 1):
            piece = part[(h - first) * step : (h - first + 1) * step]
            sums[h] = piece if sums[h] is None else sums[h] + piece
    for e in range(2):
        for h in range(height):
            value = taps_of(chans, sums[h][:, e * width : (e + 1) * width])
            spread[e, pl.ds(h, chans, stride=height), :] = value
        store(e)
    return sums


def fill(field, slot, chans, plane, borders):
    height = field.shape[0]
    at = slice(slot * chans, (slot + 1) * chans)
    for h in range(1, height - 1):
        field[h, at] = plane[(h - 1) * chans : h * chans]
    if len(borders) == 1:
        col = lax.axis_index("col")
        field[(height - 1) * col, at] = jnp.zeros_like(borders[0])
        field[(height - 1) * (1 - col), at] = borders[0]
    else:
        field[0, at] = borders[0]
        field[height - 1, at] = borders[1]


def interior_kernel(chans, height, band, joined, *rest):
    sides, (out, field, spread) = rest[:-3], rest[-3:]
    planes = joined.shape[0]
    for d in range(planes):
        fill(field, d, chans, joined[d], [side[d] for side in sides])
    for step in range(planes // 2 - 1):
        views = [lambda h, at=(2 * step + e) * chans: field[h, at : at + 3 * chans] for e in range(2)]

        def store(e):
            out[2 * step + e] = spread[step, e].astype(BF16)

        decode_pair(chans, height, band, views, spread.at[step], store)


def nearby_kernel(chans, height, took, near, far, plane, corners, spread):
    rows = plane.shape[0]

    def store(at, value):
        plane[at : at + chans] = value

    join(chans, height, took[-rows:], near, spread, store)
    start = pl.multiple_of((rows - chans) * (1 - lax.axis_index("col")), chans)
    corners[:chans] = plane[pl.ds(start, chans)]
    corners[chans:] = far[pl.ds(start, chans)]


def fill_edges(chans, joined, near, far, sides, near_rows, far_rows, field):
    planes, _, width = joined.shape
    for slot, d in ((1, 0), (2, 1), (3, planes - 2), (4, planes - 1)):
        fill(field, slot, chans, joined[d], [side[d] for side in sides])
    row, last = lax.axis_index("row"), lax.axis_size("row") - 1

    def outer(slot, plane, corners):
        fill(field, slot, chans, plane[...], corners)

    @pl.when(row % 2 == 0)
    def _():
        outer(0, far, far_rows)
        outer(5, near, near_rows)

    @pl.when(row % 2 == 1)
    def _():
        outer(0, near, near_rows)
        outer(5, far, far_rows)

    @pl.when(row == 0)
    def _():
        field[:, :chans] = jnp.zeros((field.shape[0], chans, width), BF16)

    @pl.when(row == last)
    def _():
        field[:, 5 * chans :] = jnp.zeros((field.shape[0], chans, width), BF16)


def edge_views(chans, field):
    return [lambda h, at=3 * e * chans: field[h, at : at + 3 * chans] for e in range(2)]


def result_copies(inner, held, out_hbm, sems):
    last = out_hbm.shape[0] - 1
    pieces = ((inner, out_hbm.at[1:last]), (held.at[0], out_hbm.at[0]), (held.at[1], out_hbm.at[last]))
    return [pltpu.make_async_copy(piece, place, sems.at[k]) for k, (piece, place) in enumerate(pieces)]


def edge_kernel(chans, height, band, joined, near, near_rows, far, far_rows, *rest):
    sides, (inner, out_hbm, field, spread, held, sems) = rest[:-6], rest[-6:]
    copies = result_copies(inner, held, out_hbm, sems)
    copies[0].start()
    borders = [[got[k * chans : (k + 1) * chans] for k in range(len(sides))] for got in (near_rows, far_rows)]
    fill_edges(chans, joined, near, far, sides, *borders, field)

    def store(e):
        held[e] = spread[e].astype(BF16)
        copies[1 + e].start()

    decode_pair(chans, height, band, edge_views(chans, field), spread, store)
    for copy in copies:
        copy.wait()


def early_edge_kernel(chans, height, band, joined, near, far, side, inner, values, partial, out_hbm, field, sems):
    copy = pltpu.make_async_copy(inner, out_hbm.at[1 : out_hbm.shape[0] - 1], sems.at[0])
    copy.start()
    none = [jnp.zeros((chans, joined.shape[2]), BF16)]
    fill_edges(chans, joined, near, far, [side], none, none, field)
    sums = decode_pair(chans, height, band, edge_views(chans, field), values, lambda e: None)
    partial[...] = jnp.where(lax.axis_index("col") == 0, sums[-1], sums[0])
    copy.wait()


def late_edge_kernel(chans, height, band, corners, values, partial, mid_hbm, out_hbm, window, spread, held, sems):
    copies = [
        pltpu.make_async_copy(held.at[e], out_hbm.at[d], sems.at[e])
        for e, d in ((0, 0), (1, out_hbm.shape[0] - 1))
    ]
    row, last, col = lax.axis_index("row"), lax.axis_size("row") - 1, lax.axis_index("col")
    step, width = 3 * chans, corners.shape[1]
    tile = window.shape[0]
    at_tile = pl.multiple_of((height + 2) * step // tile * tile * (1 - col), tile)
    at_row = (height + 1) * step % tile * (1 - col)
    window[...] = jnp.zeros(window.shape, BF16)

    def put(tap, got):
        window[pl.ds(pl.multiple_of(at_row + tap * chans, chans), chans), tap // 2 * width : (tap // 2 + 1) * width] = got

    even = row % 2 == 0

    @pl.when((row > 0) & even)
    def _():
        put(0, corners[chans:])

    @pl.when((row > 0) & ~even)
    def _():
        put(0, corners[:chans])

    @pl.when((row < last) & even)
    def _():
        put(2, corners[:chans])

    @pl.when((row < last) & ~even)
    def _():
        put(2, corners[chans:])

    edge = (height - 1) * (1 - col)
    kernel = band[pl.ds(pl.multiple_of(edge * step, step), step), pl.ds(at_tile, tile)]
    sums = partial[...] + dot(kernel, window[...])
    for e in range(2):
        spread[e] = values[e]
        spread[e, pl.ds(edge, chans, stride=height), :] = taps_of(chans, sums[:, e * width : (e + 1) * width])
        held[e] = spread[e].astype(BF16)
        copies[e].start()
    for copy in copies:
        copy.wait()


VMEM = pl.BlockSpec(memory_space=pltpu.MemorySpace.VMEM)
HBM = pl.BlockSpec(memory_space=pltpu.MemorySpace.HBM)


def fixed(x):
    return pltpu.with_memory_space_constraint(x, pltpu.MemorySpace.HBM)


def call(kernel, shape, ins, out, scratch=(), aliases=None, cost=0, limit=24):
    return pl.pallas_call(
        kernel,
        out_shape=shape,
        in_specs=ins,
        out_specs=out,
        scratch_shapes=list(scratch),
        input_output_aliases=aliases or {},
        cost_estimate=pl.CostEstimate(flops=cost, bytes_accessed=cost // 100, transcendentals=0),
        compiler_params=pltpu.CompilerParams(vmem_limit_bytes=limit << 20),
    )


def bf16(*shape):
    return jax.ShapeDtypeStruct(shape, BF16)


def neighbour_swaps(count, cols):
    ids = lambda row, col: row * cols + col
    first = [(ids(r, c), ids(r ^ 1, c)) for r in range(count) for c in range(cols)]
    second = []
    for r in range(count):
        for c in range(cols):
            other = r + 1 if r % 2 else r - 1
            inside = 0 <= other < count
            second.append((ids(r, c), ids(other, c) if inside else ids(r, c ^ 1)))
    return first, second


def level(features, down_weight, bott_weight, up_weight, dec_weight):
    depth, chans, height, width = features.shape
    count, cols = lax.axis_size("row"), lax.axis_size("col")
    top = down_weight.shape[4]
    coarse, rows, each = width // 8, chans * height, bott_weight.shape[3]
    feat = features.reshape(depth, rows, width)

    sems = lambda n: pltpu.SemaphoreType.DMA((n,))
    scratch = [pltpu.VMEM(feat.shape, BF16), pltpu.VMEM(down_weight.shape, BF16)]
    up_one = [(i, i + 1) for i in range(cols - 1)]
    down_one = [(i + 1, i) for i in range(cols - 1)]
    paired = cols == 2 and top // 4 == width
    if paired:
        size = top // 4
        taps = bott_weight.shape[0] * bott_weight.shape[1] * bott_weight.shape[2] * each
        lowered, keep, give = call(
            functools.partial(lower_pair_kernel, count, chans, height),
            (bf16(2 * count, coarse // 2, 4 * each), bf16(taps, size), bf16(taps + rows, size)),
            [HBM] * 3,
            (VMEM,) * 3,
            scratch + [sems(depth + 4)],
            cost=1_000_000_000,
        )(fixed(feat), fixed(down_weight), fixed(bott_weight.reshape(taps, top)))
        took = lax.ppermute(give, "row", [(i, i ^ 1) for i in range(count)])
        got = lax.all_to_all(lowered, ("row", "col"), split_axis=0, concat_axis=0, tiled=True)
        shares = call(
            bottleneck_pair_kernel,
            bf16(2 * count, coarse, size),
            [VMEM] * 3,
            VMEM,
            [pltpu.VMEM(((count + 2) * coarse, 12 * each), BF16)],
            cost=2_000_000_000,
        )(got.reshape(count, 2, coarse // 2, 4 * each), keep, took)
        parts = lax.all_to_all(shares, ("row", "col"), split_axis=0, concat_axis=0, tiled=True)
    else:
        lowered = call(
            functools.partial(lower_kernel, count, chans, height),
            bf16(count, coarse, 3 * each),
            [HBM] * 2,
            VMEM,
            scratch + [sems(depth + 1)],
            cost=1_000_000_000,
        )(fixed(feat), fixed(down_weight))
        own = lax.all_to_all(lowered, "row", split_axis=0, concat_axis=0, tiled=True)
        shares = call(
            bottleneck_kernel,
            bf16(count, coarse, top),
            [VMEM] * 4,
            VMEM,
            [pltpu.VMEM(((count + 2) * coarse, 3 * each), BF16)] * 3,
            cost=2_000_000_000,
        )(lax.ppermute(own, "col", up_one), own, lax.ppermute(own, "col", down_one), bott_weight)
        parts = lax.all_to_all(shares, "row", split_axis=0, concat_axis=0, tiled=True)

    sides = 1 if cols == 2 else 2
    wide, *ends = call(
        functools.partial(outer_kernel, chans, height),
        (bf16(4 * width, top), bf16(rows // 2 if paired else rows, width), bf16(rows, width)),
        [VMEM] * 3,
        (VMEM,) * 3,
        [pltpu.VMEM((2, rows, width), F32)],
        cost=1_000_000_000,
    )(parts, feat, up_weight)
    joined, *sides = call(
        functools.partial(raise_kernel, chans, height),
        (bf16(depth, rows, width),) + (bf16(depth + (0 if paired else 2), chans, width),) * sides,
        [VMEM] * 3,
        (VMEM,) * (1 + sides),
        [pltpu.VMEM(feat.shape, F32)],
        cost=1_000_000_000,
    )(wide, feat, up_weight)
    if cols == 2:
        sides = [lax.ppermute(sides[0], "col", up_one + down_one)]
    else:
        sides = [lax.ppermute(sides[1], "col", up_one), lax.ppermute(sides[0], "col", down_one)]

    span = rows + 2 * chans
    band = call(
        functools.partial(band_kernel, chans, height),
        bf16(3 * rows, -(-3 * span // 128) * 128),
        [VMEM, HBM],
        VMEM,
        cost=500_000_000,
    )(dec_weight, joined)

    swapped = []
    for k, pairs in enumerate(neighbour_swaps(count, cols)):
        sent = ends[k] if paired else jnp.concatenate([ends[k]] + [side[depth + k] for side in sides], axis=0)
        swapped.append(lax.ppermute(sent, ("row", "col"), pairs))
    if paired:
        plane, corners = call(
            functools.partial(nearby_kernel, chans, height),
            (bf16(rows, width), bf16(2 * chans, width)),
            [VMEM] * 3,
            (VMEM,) * 2,
            [pltpu.VMEM((rows, width), F32)],
        )(took, *swapped)
        corners = lax.ppermute(corners, "col", up_one + down_one)
    else:
        got = [part for plane in swapped for part in (plane[:rows], plane[rows:])]

    shape = bf16(depth, rows, width)
    inner = call(
        functools.partial(interior_kernel, chans, height),
        bf16(depth - 2, rows, width),
        [VMEM] * (2 + len(sides)),
        VMEM,
        [
            pltpu.VMEM((height + 2, depth * chans, width), BF16),
            pltpu.VMEM((depth // 2 - 1, 2, rows, width), F32),
        ],
        cost=3_000_000_000,
    )(band, joined, *sides)
    field = pltpu.VMEM((height + 2, 6 * chans, width), BF16)
    spread, held = pltpu.VMEM((2, rows, width), F32), pltpu.VMEM((2, rows, width), BF16)
    if paired:
        values, partial, inner = call(
            functools.partial(early_edge_kernel, chans, height),
            (jax.ShapeDtypeStruct((2, rows, width), F32), jax.ShapeDtypeStruct((3 * chans, 2 * width), F32), shape),
            [VMEM] * 6,
            (VMEM, VMEM, HBM),
            [field, sems(1)],
            cost=1_000_000_000,
        )(band, joined, plane, swapped[1], sides[0], inner)
        decoded = call(
            functools.partial(late_edge_kernel, chans, height),
            shape,
            [VMEM] * 4 + [HBM],
            HBM,
            [pltpu.VMEM((256, 2 * width), BF16), spread, held, sems(2)],
            aliases={4: 0},
            cost=1_000_000_000,
        )(band, corners, values, partial, inner)
    else:
        decoded = call(
            functools.partial(edge_kernel, chans, height),
            shape,
            [VMEM] * (7 + len(sides)),
            HBM,
            [field, spread, held, sems(3)],
            cost=1_000_000_000,
        )(band, joined, *got, *sides, inner)
    return decoded.reshape(depth, chans, height, width)


def solution(mesh):
    placed = (P("row", None, "col", None), P(), P(None, None, None, "row", None), P(), P())
    return jax.shard_map(level, mesh=mesh, in_specs=placed, out_specs=P("row", None, "col", None), check_vma=False)
```
